128 devices in a mesh: row: 16 (over y, x), col: 8 (over z, core).
Axes of the slice: x: 4, y: 4, z: 4, core: 2. Of those that a mesh axis runs over, the one named last changes fastest.
Arguments:
- coarse_kernel: bfloat16 [16, 16, 256, 256], P('row', 'col'), as said below
- interp_coef: bfloat16 [64, 2, 256, 256], P('col'), may hold values from -0.375 to 0.375
- interp_map: int32 [64, 2], replicated, may hold values from 0 to 15, as said below
- energy: float32 [16384], P(('row', 'col')), may hold values from 1 to 3
- start_vectors: float32 [256, 16384], P(None, ('row', 'col')), may hold values from -6 to 6
Outputs:
- second: float32 [256, 16384], P(None, ('row', 'col'))
- residual: float32 [256, 16384], P(None, ('row', 'col'))
- coeffs: float32 [3, 256], replicated
- kernel: bfloat16 [16384, 16384], P('row', 'col')
The draws below stay inside these ranges and needn't reach their ends.
Inputs may be any that keep to these rules, and one draw needn't show every extreme that they name: coarse_kernel[a, b] is the transpose of coarse_kernel[b, a], so the kernel is symmetric. interp_map[i, 0] is i // 4; interp_map[i, 1] is interp_map[i, 0] - 1 or interp_map[i, 0] + 1 modulo 16: the first where i % 4 == 0, the second where i % 4 == 3.
All inputs are finite; a program needn't handle non-finite values.
Results may differ from the reference program's by a relative error of at most 0.0052.
Values may be sent and summed in bfloat16 or wider, within the bound.
A program may use at most 64 MiB of HBM per device.

```python
import jax
import jax.numpy as jnp
from jax import lax

BANDS = 256
NVEC = 256
KR = 4
NEIGH = 2
NK = 64
NC = 16
ORDER = 16384


def draw_coarse_kernel(key, part):
    raw = jax.random.normal(key, (NC, NC, BANDS, BANDS), jnp.float32)
    mirrored = (raw + jnp.transpose(raw, (1, 0, 3, 2))) * 0.5 ** 0.5
    return (mirrored * (0.5 / (NK * BANDS) ** 0.5)).astype(jnp.bfloat16)


def draw_interp_map(key, part):
    fine_index = jnp.arange(NK, dtype=jnp.int32)
    home = fine_index // KR
    place = fine_index % KR
    coin = jax.random.randint(jax.random.fold_in(key, 7), (NK,), 0, 2).astype(jnp.int32) * 2 - 1
    offset = jnp.where(place == 0, -1, jnp.where(place == KR - 1, 1, coin)).astype(jnp.int32)
    other = (home + offset + NC) % NC
    return jnp.stack([home, other], axis=1).astype(jnp.int32)


def levels(key, dims, split, least, largest):
    def one(position, parts):
        heights = jax.random.uniform(jax.random.fold_in(jax.random.fold_in(key, 6), position), (parts,), jnp.float32, least / len(split), largest / len(split))
        return jnp.repeat(jnp.exp(heights), dims[position] // parts).reshape((-1,) + (1,) * (len(dims) - position - 1))

    factor_of = one(*split[0])
    for cut in split[1:]:
        factor_of = factor_of * one(*cut)
    return factor_of


def noise(key, dims, spread, most, split=(), kind=jnp.bfloat16):
    result = spread * jax.random.normal(key, dims, jnp.float32)
    if split:
        result = result * levels(key, dims, split, -0.22, 0.18)
    return jnp.clip(result, -most, most).astype(kind)


def setup_inputs(seed: int = 0) -> dict:
    key_list = jax.random.split(jax.random.key(seed), 6)
    return {
        "coarse_kernel": draw_coarse_kernel(jax.random.fold_in(key_list[5], 71), 0),
        "interp_coef": noise(key_list[1], (NK, NEIGH, BANDS, BANDS), BANDS ** -0.5, 0.375, ((0, 8),)),
        "interp_map": draw_interp_map(jax.random.fold_in(key_list[5], 71), 0),
        "energy": jnp.clip(1.0 + 2.0 * jax.random.uniform(key_list[3], (ORDER,), jnp.float32) ** levels(key_list[3], (ORDER,), ((0, 128),), -0.2, 0.2), 1.0, 3.0),
        "start_vectors": noise(key_list[4], (NVEC, ORDER), 1.0, 6.0, ((1, 128),), jnp.float32),
    }


EPS = 1e-06

def right_factor(coarse_kernel, interp_coef, interp_map):
    summed = jnp.zeros((NC, NK, BANDS, BANDS), jnp.float32)
    for neighbor in range(NEIGH):
        picked = jnp.take(coarse_kernel, interp_map[:, neighbor], axis=1).astype(jnp.float32)
        summed = summed + jnp.einsum('ajxy,jyz->ajxz', picked, interp_coef[:, neighbor].astype(jnp.float32))
    return summed.astype(jnp.bfloat16)

def kernel_rows(right_part, interp_coef, interp_map):

    def one_row(packed):
        coefs, which = packed
        summed = jnp.zeros((NK, BANDS, BANDS), jnp.float32)
        for neighbor in range(NEIGH):
            strip = lax.dynamic_index_in_dim(right_part, which[neighbor], 0, keepdims=False).astype(jnp.float32)
            summed = summed + jnp.einsum('xy,jxz->jyz', coefs[neighbor].astype(jnp.float32), strip)
        blocks = summed.astype(jnp.bfloat16)
        return jnp.transpose(blocks, (1, 0, 2)).reshape(BANDS, NK * BANDS)
    return lax.map(one_row, (interp_coef, interp_map))

def apply_operator(rows, energy, vectors):
    packed = vectors.astype(jnp.bfloat16)

    def one_block(row_block):
        return jnp.dot(packed, row_block.T, preferred_element_type=jnp.float32)
    pieces = lax.map(one_block, rows)
    return jnp.transpose(pieces, (1, 0, 2)).reshape(NVEC, NK * BANDS) + energy[None, :] * vectors

def reference(coarse_kernel, interp_coef, interp_map, energy, start_vectors):
    right_part = right_factor(coarse_kernel, interp_coef, interp_map)
    rows = kernel_rows(right_part, interp_coef, interp_map)
    scaling = jnp.sqrt(lax.optimization_barrier(jnp.mean(start_vectors * start_vectors, axis=1)) + EPS)
    first = start_vectors / scaling[:, None]
    image_one = apply_operator(rows, energy, first)
    alpha_one = lax.optimization_barrier(jnp.mean(first * image_one, axis=1))
    remain = image_one - alpha_one[:, None] * first
    beta_one = jnp.sqrt(lax.optimization_barrier(jnp.mean(remain * remain, axis=1)) + EPS)
    second = remain / beta_one[:, None]
    image_two = apply_operator(rows, energy, second)
    shifted = image_two - beta_one[:, None] * first
    alpha_two = lax.optimization_barrier(jnp.mean(second * shifted, axis=1))
    residual = shifted - alpha_two[:, None] * second
    kernel = rows.reshape(NK * BANDS, NK * BANDS)
    return (second, residual, jnp.stack([alpha_one, beta_one, alpha_two]), kernel)
```

```python
import jax
import jax.numpy as jnp
from jax import lax
from jax.experimental import pallas as pl
from jax.experimental.pallas import tpu as pltpu
from jax.sharding import PartitionSpec as P

ROWS = 16
COLS = 8
BANDS = 256
NVEC = 256
FINE = 8
KR = 4
VS = NVEC // ROWS
HALF = 128
ORDER = 16384
EPS = 1e-06
PRESCALE = 0.125
SHIFT = 2.0

F32 = jnp.float32
BF16 = jnp.bfloat16
MESH = pl.DeviceIdType.MESH

NT = (((1,), (1,)), ((), ()))
NN = (((1,), (0,)), ((), ()))


def mm(a, b, dims):
    return lax.dot_general(a, b, dims, preferred_element_type=F32)


def wait_bytes(ref, sem):
    pltpu.make_async_copy(ref, ref, sem).wait()


def kernel(
    map_ref, kc_ref, coef_ref, e_ref, s_ref,
    second_ref, resid_ref, coeffs_ref, tile_ref,
    scol, ecol, gcol, kbuf, ci, cit, lbuf, tbuf,
    hw_send, hw_recv, wsend, wfull, usend, ured, hu_send, hu_recv,
    zs_send, zs_recv, sec_send, sec_nat, sh_send, sh_nat, cf_send, cf_recv,
    ssem, rsem, tsem,
):
    r = lax.axis_index("row")
    c = lax.axis_index("col")
    z = lax.div(c, 2)
    k = lax.rem(c, 2)
    x = lax.rem(r, 4)
    y = lax.div(r, 4)
    diag_col = lax.div(r, 2)
    is_diag = c == diag_col
    c_prev = lax.rem(c + COLS - 1, COLS)
    c_next = lax.rem(c + 1, COLS)
    finish = []

    def remote(src, dst, sem, tr, tc):
        pltpu.make_async_remote_copy(
            src_ref=src, dst_ref=dst, send_sem=ssem.at[sem], recv_sem=rsem.at[sem],
            device_id=(tr, tc), device_id_type=MESH,
        ).start()

    def local(src, dst, sem):
        pltpu.make_async_copy(src, dst, rsem.at[sem]).start()

    def maybe_self(src, dst, sem, tr, tc):
        @pl.when(is_diag)
        def _():
            local(src, dst, sem)

        @pl.when(jnp.logical_not(is_diag))
        def _():
            remote(src, dst, sem, tr, tc)

    def finish_diag(sem, buf):
        def run():
            @pl.when(is_diag)
            def _():
                wait_bytes(buf.at[pl.ds(0, 15)], ssem.at[sem])

            @pl.when(jnp.logical_not(is_diag))
            def _():
                wait_bytes(buf, ssem.at[sem])

        finish.append(run)

    def finish_plain(sem, buf):
        finish.append(lambda: wait_bytes(buf, ssem.at[sem]))

    S, E, KH, CA, CB = 0, 1, 2, 3, 4
    base = 5

    for t in range(ROWS):
        tr = lax.rem(r + t, ROWS)
        src = s_ref.at[pl.ds(pl.multiple_of(tr * VS, VS), VS), :]
        dst = scol.at[lax.rem(r, 2) * COLS + c]
        (maybe_self if t == 0 else remote)(src, dst, S, tr, diag_col)
    finish_diag(S, scol)
    for t in range(ROWS):
        tr = lax.rem(r + t, ROWS)
        dst = ecol.at[lax.rem(r, 2) * COLS + c]
        (maybe_self if t == 0 else remote)(e_ref, dst, E, tr, diag_col)
    finish_diag(E, ecol)

    serves = lax.div(x, 2) == k
    delta = lax.rem(y - z + 4, 4)
    mine = lax.rem(x, 2) * KR + delta
    for t in range(1, 4):
        tz = lax.rem(z + t, 4)

        @pl.when(serves)
        def _(tz=tz):
            remote(coef_ref.at[mine], ci.at[delta], CA, 4 * z + x, 2 * tz + lax.div(delta, 2))

    for dr in (1, ROWS - 1):
        tr = lax.rem(r + dr, ROWS)
        slot = 0 if dr == 1 else 2
        remote(kc_ref.at[0], kbuf.at[pl.ds(4 * slot + 1, 2)], KH, tr, c)
    for dr in (0, 1, ROWS - 1):
        tr = lax.rem(r + dr, ROWS)
        slot = {0: 1, 1: 0, ROWS - 1: 2}[dr]
        remote(kc_ref.at[0, 0], kbuf.at[4 * slot + 3], KH, tr, c_prev)
        remote(kc_ref.at[0, 1], kbuf.at[4 * slot], KH, tr, c_next)
    for b in range(2):
        kbuf[5 + b] = kc_ref[0, b]
    finish_plain(KH, kbuf.at[pl.ds(0, 10)])

    plus = []
    for j in range(FINE):
        home = c * 2 + j // KR
        flag = map_ref[c * FINE + j, 1] == lax.rem(home + 1, ROWS)
        plus.append(flag.astype(F32))

    def restrict(parts, app):
        acc = [jnp.zeros((VS, BANDS), F32) for _ in range(4)]
        for j in range(FINE):
            home = 1 + j // KR
            own = parts[j].astype(BF16)
            up = parts[j] * plus[j]
            both = jnp.concatenate([parts[j] - up, up], axis=0).astype(BF16)
            acc[home] = acc[home] + mm(own, coef_ref[j, 0], NT)
            side = mm(both, coef_ref[j, 1], NT)
            acc[home - 1] = acc[home - 1] + side[:VS]
            acc[home + 1] = acc[home + 1] + side[VS:]
        sem = base + 8 * app
        hw_send[app, 0] = acc[0].astype(BF16)
        hw_send[app, 1] = acc[3].astype(BF16)
        remote(hw_send.at[app, 0], hw_recv.at[app, 1], sem, r, c_prev)
        remote(hw_send.at[app, 1], hw_recv.at[app, 0], sem, r, c_next)
        finish_plain(sem, hw_send.at[app])
        wait_bytes(hw_recv.at[app], rsem.at[sem])
        w0 = acc[1] + hw_recv[app, 0].astype(F32)
        w1 = acc[2] + hw_recv[app, 1].astype(F32)
        wsend[app] = jnp.concatenate([w0, w1], axis=1).astype(BF16)

    def gather_plane(app):
        sem = base + 8 * app + 1
        local(wsend.at[app], wfull.at[app, r], sem)
        for t in range(1, ROWS):
            remote(wsend.at[app], wfull.at[app, r], sem, lax.rem(r + t, ROWS), c)
        finish_plain(sem, wfull.at[app, pl.ds(0, 15)])

    def coarse_apply(app):
        wait_bytes(wfull.at[app], rsem.at[base + 8 * app + 1])
        full = wfull[app].reshape(NVEC, 2 * BANDS)
        part = mm(full[:, :BANDS], kc_ref[0, 0], NT) + mm(full[:, BANDS:], kc_ref[0, 1], NT)
        usend[app] = part.astype(BF16).reshape(ROWS, VS, BANDS)
        sem = base + 8 * app + 2
        for t in range(ROWS):
            tr = lax.rem(r + t, ROWS)
            dst = ured.at[app, lax.rem(r, 2) * COLS + c]
            (maybe_self if t == 0 else remote)(usend.at[app, tr], dst, sem, tr, diag_col)
        finish_diag(sem, usend.at[app])

    def reduce_coarse(app):
        wait_bytes(ured.at[app], rsem.at[base + 8 * app + 2])
        u = []
        for h in range(2):
            total = ured[app, h * COLS].astype(F32)
            for t in range(1, COLS):
                total = total + ured[app, h * COLS + t].astype(F32)
            u.append(total)
        sem = base + 8 * app + 3
        for h in range(2):
            hu_send[app, h] = u[h].astype(BF16)
        remote(hu_send.at[app, 0], hu_recv.at[app, 1], sem, r, c_prev)
        remote(hu_send.at[app, 1], hu_recv.at[app, 0], sem, r, c_next)
        finish_plain(sem, hu_send.at[app])
        wait_bytes(hu_recv.at[app], rsem.at[sem])
        return [hu_recv[app, 0].astype(F32), u[0], u[1], hu_recv[app, 1].astype(F32)]

    def prolong(u, j):
        home = 1 + j // KR
        side = u[home - 1] * (1.0 - plus[j]) + u[home + 1] * plus[j]
        return mm(u[home].astype(BF16), coef_ref[j, 0], NN) + mm(side.astype(BF16), coef_ref[j, 1], NN)

    def exchange_sums(app, message):
        sem = base + 8 * app + 4
        zs_send[app] = message
        local(zs_send.at[app], zs_recv.at[app, c], sem)
        for t in range(1, COLS):
            remote(zs_send.at[app], zs_recv.at[app, c], sem, r, lax.rem(c + t, COLS))
        finish_plain(sem, zs_recv.at[app, pl.ds(0, 7)])

    def sums(app):
        wait_bytes(zs_recv.at[app], rsem.at[base + 8 * app + 4])
        total = zs_recv[app, 0]
        for t in range(1, COLS):
            total = total + zs_recv[app, t]
        return total

    def to_native(src, dst, sem):
        start = lax.rem(r, 2) * COLS + c
        for t in range(ROWS):
            q = lax.rem(start + t, ROWS)
            tr = 2 * c + lax.div(q, COLS)
            tc = lax.rem(q, COLS)
            (maybe_self if t == 0 else remote)(src.at[q], dst.at[r], sem, tr, tc)
        finish_diag(sem, src)

    lanes = lax.broadcasted_iota(jnp.int32, (VS, HALF), 1)

    def s_block(j):
        return jnp.concatenate([scol[2 * j], scol[2 * j + 1]], axis=1) * PRESCALE

    def d_block(j):
        return jnp.concatenate([ecol[2 * j], ecol[2 * j + 1]], axis=1) - SHIFT

    def row_sum(v):
        return jnp.sum(v, axis=1, keepdims=True)

    wait_bytes(scol, rsem.at[S])
    restrict([s_block(j) for j in range(FINE)], 0)
    gather_plane(0)

    sibling = 2 * z + (1 - k)
    at_source = z == y
    home_core = lax.div(x, 2)
    local_at = lax.rem(x, 2) * KR

    @pl.when(jnp.logical_not(at_source))
    def _():
        mine_pair = ci.at[pl.ds(2 * k, 2)]
        wait_bytes(mine_pair, rsem.at[CA])
        remote(mine_pair, mine_pair, CB, r, sibling)

    @pl.when(jnp.logical_and(at_source, k == home_core))
    def _():
        pltpu.make_async_copy(coef_ref.at[pl.ds(local_at, KR)], ci, rsem.at[CA]).start()
        remote(coef_ref.at[pl.ds(local_at, KR)], ci, CB, r, sibling)
        wait_bytes(ci, rsem.at[CA])

    coarse_apply(0)

    @pl.when(jnp.logical_not(at_source))
    def _():
        wait_bytes(ci.at[pl.ds(0, 2)], rsem.at[CB])

    @pl.when(jnp.logical_and(at_source, k != home_core))
    def _():
        wait_bytes(ci, rsem.at[CB])

    wait_bytes(kbuf.at[pl.ds(0, 10)], rsem.at[KH])
    for i in range(KR):
        for n in range(2):
            cit[i, n] = ci[i, n].T

    up_row = []
    for i in range(KR):
        flag = map_ref[r * KR + i, 1] == lax.rem(r + 1, ROWS)
        up_row.append(jnp.where(flag, 8, 0))
    for i in range(KR):
        for b in range(4):
            value = mm(cit[i, 0], kbuf[4 + b], NN) + mm(cit[i, 1], kbuf[up_row[i] + b], NN)
            lbuf[b, pl.ds(i * BANDS, BANDS), :] = value.astype(BF16)

    def tile_piece(j):
        home = 1 + j // KR
        flag = map_ref[c * FINE + j, 1] == lax.rem(c * 2 + j // KR + 1, ROWS)
        other = jnp.where(flag, home + 1, home - 1)
        for m in range(KR):
            rows = pl.ds(m * BANDS, BANDS)
            value = mm(lbuf[home, rows], coef_ref[j, 0], NN) + mm(lbuf[other, rows], coef_ref[j, 1], NN)
            tbuf[j, rows, :] = value.astype(BF16)
        pltpu.make_async_copy(
            tbuf.at[j], tile_ref.at[:, pl.ds(j * BANDS, BANDS)], tsem.at[j]
        ).start()

    u = reduce_coarse(0)
    wait_bytes(ecol, rsem.at[E])
    parts = []
    ss = sg = gg = jnp.zeros((VS, 1), F32)
    for j in range(FINE):
        s_j = s_block(j)
        g_j = prolong(u, j) + d_block(j) * s_j
        gcol[j] = g_j
        parts.append(g_j)
        ss = ss + row_sum(s_j * s_j)
        sg = sg + row_sum(s_j * g_j)
        gg = gg + row_sum(g_j * g_j)
    restrict(parts, 1)
    gather_plane(1)
    exchange_sums(0, jnp.where(lanes == 0, ss, jnp.where(lanes == 1, sg, gg)))
    for j in range(4):
        tile_piece(j)
    coarse_apply(1)

    mean = sums(0) / ORDER
    ss, sg, gg = mean[:, 0:1], mean[:, 1:2], mean[:, 2:3]
    var = ss + EPS * PRESCALE * PRESCALE
    scale = jnp.sqrt(var)
    alpha_one = (sg + SHIFT * ss) / var
    mix = SHIFT - alpha_one
    remain_sq = (gg + 2.0 * mix * sg + mix * mix * ss) / var
    beta = jnp.sqrt(jnp.maximum(remain_sq, 0.0) + EPS)
    inv = 1.0 / (scale * beta)
    for j in range(FINE):
        sec = (gcol[j] + mix * s_block(j)) * inv
        for h in range(2):
            sec_send[2 * j + h] = sec[:, h * HALF:(h + 1) * HALF]
    to_native(sec_send, sec_nat, base + 5)
    for j in range(4, FINE):
        tile_piece(j)

    u = reduce_coarse(1)
    over = beta / scale
    dot = jnp.zeros((VS, 1), F32)
    for j in range(FINE):
        s_j = s_block(j)
        g_j = gcol[j]
        h_j = prolong(u, j) + d_block(j) * g_j
        sec = jnp.concatenate([sec_send[2 * j], sec_send[2 * j + 1]], axis=1)
        shifted = (h_j + mix * g_j) * inv + SHIFT * sec - over * s_j
        dot = dot + row_sum(sec * shifted)
        for h in range(2):
            sh_send[2 * j + h] = shifted[:, h * HALF:(h + 1) * HALF]
    exchange_sums(1, jnp.broadcast_to(dot, (VS, HALF)))
    to_native(sh_send, sh_nat, base + 6)

    alpha_two = sums(1) / ORDER
    cf_send[...] = jnp.where(lanes == 0, alpha_one, jnp.where(lanes == 1, beta, alpha_two))
    sem = base + 7
    local(cf_send, cf_recv.at[r], sem)
    for t in range(1, ROWS):
        remote(cf_send, cf_recv.at[r], sem, lax.rem(r + t, ROWS), c)
    finish_plain(sem, cf_recv.at[pl.ds(0, 15)])

    wait_bytes(sec_nat, rsem.at[base + 5])
    sec = sec_nat[...].reshape(NVEC, HALF)
    second_ref[...] = sec
    wait_bytes(sh_nat, rsem.at[base + 6])
    wait_bytes(cf_recv, rsem.at[base + 7])
    coefs = cf_recv[...].reshape(NVEC, HALF)
    resid_ref[...] = sh_nat[...].reshape(NVEC, HALF) - coefs[:, 2:3] * sec
    coeffs_ref[...] = coefs.T[0:8]

    for j in range(FINE):
        pltpu.make_async_copy(
            tbuf.at[j], tile_ref.at[:, pl.ds(j * BANDS, BANDS)], tsem.at[j]
        ).wait()

    @pl.when(serves)
    def _():
        wait_bytes(coef_ref.at[pl.ds(0, 3)], ssem.at[CA])

    @pl.when(jnp.logical_not(at_source))
    def _():
        wait_bytes(ci.at[pl.ds(0, 2)], ssem.at[CB])

    @pl.when(jnp.logical_and(at_source, k == home_core))
    def _():
        wait_bytes(ci, ssem.at[CB])

    for run in finish:
        run()


def per_device(coarse_kernel, interp_coef, interp_map, energy, start_vectors):
    vmem = pl.BlockSpec(memory_space=pltpu.VMEM)
    nsem = 5 + 16
    second, residual, coeffs, tile = pl.pallas_call(
        kernel,
        out_shape=(
            jax.ShapeDtypeStruct((NVEC, HALF), F32),
            jax.ShapeDtypeStruct((NVEC, HALF), F32),
            jax.ShapeDtypeStruct((8, NVEC), F32),
            jax.ShapeDtypeStruct((KR * BANDS, FINE * BANDS), BF16),
        ),
        in_specs=[pl.BlockSpec(memory_space=pltpu.SMEM), vmem, vmem, vmem, vmem],
        out_specs=(vmem, vmem, vmem, pl.BlockSpec(memory_space=pl.ANY)),
        scratch_shapes=[
            pltpu.VMEM((16, VS, HALF), F32),
            pltpu.VMEM((16, 1, HALF), F32),
            pltpu.VMEM((FINE, VS, BANDS), F32),
            pltpu.VMEM((12, BANDS, BANDS), BF16),
            pltpu.VMEM((KR, 2, BANDS, BANDS), BF16),
            pltpu.VMEM((KR, 2, BANDS, BANDS), BF16),
            pltpu.VMEM((4, KR * BANDS, BANDS), BF16),
            pltpu.VMEM((FINE, KR * BANDS, BANDS), BF16),
            pltpu.VMEM((2, 2, VS, BANDS), BF16),
            pltpu.VMEM((2, 2, VS, BANDS), BF16),
            pltpu.VMEM((2, VS, 2 * BANDS), BF16),
            pltpu.VMEM((2, ROWS, VS, 2 * BANDS), BF16),
            pltpu.VMEM((2, ROWS, VS, BANDS), BF16),
            pltpu.VMEM((2, 16, VS, BANDS), BF16),
            pltpu.VMEM((2, 2, VS, BANDS), BF16),
            pltpu.VMEM((2, 2, VS, BANDS), BF16),
            pltpu.VMEM((2, VS, HALF), F32),
            pltpu.VMEM((2, COLS, VS, HALF), F32),
            pltpu.VMEM((16, VS, HALF), F32),
            pltpu.VMEM((16, VS, HALF), F32),
            pltpu.VMEM((16, VS, HALF), F32),
            pltpu.VMEM((16, VS, HALF), F32),
            pltpu.VMEM((VS, HALF), F32),
            pltpu.VMEM((16, VS, HALF), F32),
            pltpu.SemaphoreType.DMA((nsem,)),
            pltpu.SemaphoreType.DMA((nsem,)),
            pltpu.SemaphoreType.DMA((FINE,)),
        ],
        compiler_params=pltpu.CompilerParams(
            has_side_effects=True, vmem_limit_bytes=40 * 1024 * 1024
        ),
    )(interp_map, coarse_kernel, interp_coef, energy.reshape(1, HALF), start_vectors)
    return second, residual, coeffs[:3], tile


def solution(mesh):
    return jax.shard_map(
        per_device,
        mesh=mesh,
        in_specs=(
            P("row", "col", None, None),
            P("col", None, None, None),
            P(),
            P(("row", "col")),
            P(None, ("row", "col")),
        ),
        out_specs=(P(None, ("row", "col")), P(None, ("row", "col")), P(), P("row", "col")),
        check_vma=False,
    )
```

```python
import jax
import jax.numpy as jnp
from jax import lax
from jax.experimental import pallas as pl
from jax.experimental.pallas import tpu as pltpu
from jax.sharding import PartitionSpec as P

ROWS = 16
COLS = 8
BANDS = 256
NVEC = 256
FINE = 8
KR = 4
VS = NVEC // ROWS
HALF = 128
ORDER = 16384
EPS = 1e-06
PRESCALE = 0.125
SHIFT = 2.0

F32 = jnp.float32
BF16 = jnp.bfloat16
MESH = pl.DeviceIdType.MESH

NT = (((1,), (1,)), ((), ()))
NN = (((1,), (0,)), ((), ()))

OFFSETS = sorted(
    ((dy, dx) for dy in range(4) for dx in range(4)),
    key=lambda t: -(min(t[0], 4 - t[0]) + min(t[1], 4 - t[1])),
)
AROUND = (4, 2, 6, 3, 5, 1, 7, 0)


def mm(a, b, dims):
    return lax.dot_general(a, b, dims, preferred_element_type=F32)


def wait_bytes(ref, sem):
    pltpu.make_async_copy(ref, ref, sem).wait()


def kernel(
    map_ref, kc_hbm, coef_hbm, e_hbm, s_hbm,
    second_ref, resid_ref, coeffs_ref, tile_ref,
    kc_ref, coef_ref, e_ref, s_ref,
    scol, ecol, gcol, kbuf, ci, cit, lbuf, tbuf,
    wsend, wside, wfull, wlow, whigh, usend, ured,
    zs_send, zs_recv, ab_send, ab_recv, sec_send, sec_nat, sh_send, sh_nat, dot_send, dot_recv,
    ssem, rsem, tsem, lsem,
):
    r = lax.axis_index("row")
    c = lax.axis_index("col")
    z = lax.div(c, 2)
    k = lax.rem(c, 2)
    x = lax.rem(r, 4)
    y = lax.div(r, 4)
    odd = lax.rem(r, 2)
    c_prev = lax.rem(c + COLS - 1, COLS)
    c_next = lax.rem(c + 1, COLS)
    diag_col = lax.div(r, 2)
    near_col = lax.rem(diag_col + COLS - 1 + 2 * odd, COLS)
    is_diag = c == diag_col
    is_near = c == near_col
    first_row = 2 * c
    sibling = 2 * z + (1 - k)
    finish = []

    loads = []
    for n, (src, dst) in enumerate(((s_hbm, s_ref), (e_hbm, e_ref), (kc_hbm, kc_ref), (coef_hbm, coef_ref))):
        loads.append(pltpu.make_async_copy(src, dst, lsem.at[n]))
        loads[-1].start()

    barrier = pltpu.get_barrier_semaphore()

    def greet(tr, tc):
        pl.semaphore_signal(barrier, inc=1, device_id=(tr, tc), device_id_type=MESH)

    def plane_row(t):
        dy, dx = t
        return 4 * lax.rem(y + dy, 4) + lax.rem(x + dx, 4)

    for tz in AROUND:
        for t in OFFSETS:
            if tz or t != (0, 0):
                greet(plane_row(t), lax.rem(c + tz, COLS))
    pl.semaphore_wait(barrier, ROWS * COLS - 1)

    def remote(src, dst, sem, tr, tc):
        pltpu.make_async_remote_copy(
            src_ref=src, dst_ref=dst, send_sem=ssem.at[sem], recv_sem=rsem.at[sem],
            device_id=(tr, tc), device_id_type=MESH,
        ).start()

    def local(src, dst, sem):
        pltpu.make_async_copy(src, dst, rsem.at[sem]).start()

    def either(here, src, dst, sem, tr, tc):
        @pl.when(here)
        def _():
            local(src, dst, sem)

        @pl.when(jnp.logical_not(here))
        def _():
            remote(src, dst, sem, tr, tc)

    def finish_plain(sem, buf):
        finish.append(lambda: wait_bytes(buf, ssem.at[sem]))

    def finish_but_one(here, sem, buf, count):
        def run():
            @pl.when(here)
            def _():
                wait_bytes(buf.at[pl.ds(0, count - 1)], ssem.at[sem])

            @pl.when(jnp.logical_not(here))
            def _():
                wait_bytes(buf.at[pl.ds(0, count)], ssem.at[sem])

        finish.append(run)

    S, E, K1, K2, CA, CR, CB, AB, SEC, SH, DOT, ZS, APP = range(13)

    loads[0].wait()
    loads[1].wait()
    for t in OFFSETS:
        tr = plane_row(t)
        src = s_ref.at[pl.ds(pl.multiple_of(tr * VS, VS), VS), :]
        dst = scol.at[odd * COLS + c]
        if t == (0, 0):
            either(is_diag, src, dst, S, tr, diag_col)
        else:
            remote(src, dst, S, tr, diag_col)
    finish_but_one(is_diag, S, scol, ROWS)
    for t in OFFSETS:
        tr = plane_row(t)
        dst = ecol.at[odd * COLS + c]
        if t == (0, 0):
            either(is_diag, e_ref, dst, E, tr, diag_col)
        else:
            remote(e_ref, dst, E, tr, diag_col)
    finish_but_one(is_diag, E, ecol, ROWS)
    loads[2].wait()
    loads[3].wait()

    serves = lax.div(x, 2) == k
    delta = lax.rem(y - z + 4, 4)
    mine = lax.rem(x, 2) * KR + delta
    away = lax.rem(z - y + 4, 4)
    at_source = away == 0
    home_core = lax.div(x, 2)
    is_home = jnp.logical_and(at_source, k == home_core)
    direct = jnp.logical_or(away == 1, away == 3)
    r_next = lax.rem(r + 1, ROWS)
    r_prev = lax.rem(r + ROWS - 1, ROWS)
    pair = pl.ds(2 * k, 2)

    def bulk_direct(b):
        remote(kc_ref.at[0, b], kbuf.at[1 + b], K1, r_next, c)
        remote(kc_ref.at[0, b], kbuf.at[9 + b], K1, r_prev, c)

        @pl.when(serves)
        def _():
            for t in (1, 3):
                remote(
                    coef_ref.at[mine, b], ci.at[delta, b], CA,
                    4 * z + x, 2 * lax.rem(z + t, 4) + lax.div(delta, 2),
                )

    def bulk_second():
        wait_bytes(kbuf.at[pl.ds(0, 4)], rsem.at[K1])
        for slot in range(3):
            remote(kbuf.at[4 * slot + 1], kbuf.at[4 * slot + 3], K2, r, c_prev)
            remote(kbuf.at[4 * slot + 2], kbuf.at[4 * slot], K2, r, c_next)

        @pl.when(direct)
        def _():
            wait_bytes(ci.at[pl.ds(0, 2)], rsem.at[CA])

        @pl.when(away == 1)
        def _():
            remote(ci.at[pair, 0], ci.at[pair, 0], CR, r, 2 * lax.rem(z + 1, 4) + k)

        @pl.when(away == 3)
        def _():
            remote(ci.at[pair, 1], ci.at[pair, 1], CR, r, 2 * lax.rem(z + 3, 4) + k)

    def bulk_siblings():
        @pl.when(away == 2)
        def _():
            wait_bytes(ci.at[pl.ds(0, 2)], rsem.at[CR])

        @pl.when(jnp.logical_not(at_source))
        def _():
            remote(ci.at[pair], ci.at[pair], CB, r, sibling)

        @pl.when(is_home)
        def _():
            src = coef_ref.at[pl.ds(odd * KR, KR)]
            local(src, ci, CA)
            remote(src, ci, CB, r, sibling)

    def bulk_wait():
        @pl.when(is_home)
        def _():
            wait_bytes(ci, rsem.at[CA])

        @pl.when(jnp.logical_not(at_source))
        def _():
            wait_bytes(ci.at[pl.ds(0, 2)], rsem.at[CB])

        @pl.when(jnp.logical_and(at_source, k != home_core))
        def _():
            wait_bytes(ci, rsem.at[CB])

        wait_bytes(kbuf.at[pl.ds(0, 6)], rsem.at[K2])

    def bulk_finish():
        wait_bytes(kbuf.at[pl.ds(0, 4)], ssem.at[K1])
        wait_bytes(kbuf.at[pl.ds(0, 6)], ssem.at[K2])

        @pl.when(serves)
        def _():
            wait_bytes(ci.at[pl.ds(0, 2)], ssem.at[CA])

        @pl.when(direct)
        def _():
            wait_bytes(ci.at[0], ssem.at[CR])

        @pl.when(jnp.logical_not(at_source))
        def _():
            wait_bytes(ci.at[pl.ds(0, 2)], ssem.at[CB])

        @pl.when(is_home)
        def _():
            wait_bytes(ci, ssem.at[CB])

    finish.append(bulk_finish)
    bulk_direct(0)
    for b in range(2):
        kbuf[5 + b] = kc_ref[0, b]

    plus = []
    for j in range(FINE):
        home = c * 2 + j // KR
        flag = map_ref[1, c * FINE + j] == lax.rem(home + 1, ROWS)
        plus.append(flag.astype(F32))

    def split(v):
        high = v.astype(BF16)
        return high, (v - high.astype(F32)).astype(BF16)

    def restrict(parts, app):
        acc = [jnp.zeros((VS, BANDS), F32) for _ in range(4)]
        for j in range(FINE):
            home = 1 + j // KR
            high, low = split(parts[j])
            both = jnp.concatenate([high, low], axis=0)
            up = (both.astype(F32) * plus[j]).astype(BF16)
            down = both - up
            own = mm(both, coef_ref[j, 0], NT)
            side = mm(jnp.concatenate([down, up], axis=0), coef_ref[j, 1], NT)
            acc[home] = acc[home] + own[:VS] + own[VS:]
            acc[home - 1] = acc[home - 1] + side[:VS] + side[VS:2 * VS]
            acc[home + 1] = acc[home + 1] + side[2 * VS:3 * VS] + side[3 * VS:]
        wsend[app] = jnp.concatenate([acc[1], acc[2]], axis=1).astype(BF16)
        wside[app, 0] = acc[0].astype(BF16)
        wside[app, 1] = acc[3].astype(BF16)
        sem = APP + 4 * app
        for t in OFFSETS:
            tr = plane_row(t)
            remote(wside.at[app, 0], whigh.at[app, r], sem, tr, c_prev)
            remote(wside.at[app, 1], wlow.at[app, r], sem + 1, tr, c_next)
            if t == (0, 0):
                local(wsend.at[app], wfull.at[app, r], sem + 2)
            else:
                remote(wsend.at[app], wfull.at[app, r], sem + 2, tr, c)
        finish_plain(sem, whigh.at[app])
        finish_plain(sem + 1, wlow.at[app])
        finish_plain(sem + 2, wfull.at[app, pl.ds(0, ROWS - 1)])

    def coarse_apply(app):
        sem = APP + 4 * app
        wait_bytes(wfull.at[app], rsem.at[sem + 2])
        wait_bytes(whigh.at[app], rsem.at[sem])
        wait_bytes(wlow.at[app], rsem.at[sem + 1])
        full = wfull[app].reshape(NVEC, 2 * BANDS)
        left = full[:, :BANDS].astype(F32) + wlow[app].reshape(NVEC, BANDS).astype(F32)
        right = full[:, BANDS:].astype(F32) + whigh[app].reshape(NVEC, BANDS).astype(F32)
        part = mm(left.astype(BF16), kc_ref[0, 0], NT) + mm(right.astype(BF16), kc_ref[0, 1], NT)
        usend[app] = part.astype(BF16).reshape(ROWS, VS, BANDS)
        for t in OFFSETS:
            tr = plane_row(t)
            src = usend.at[app, tr]
            own = ured.at[app, (1 + odd) * COLS + c]
            near = ured.at[app, 3 * (1 - odd) * COLS + c]
            if t == (0, 0):
                either(is_diag, src, own, sem + 3, tr, diag_col)
                either(is_near, src, near, sem + 3, tr, near_col)
            else:
                remote(src, own, sem + 3, tr, diag_col)
                remote(src, near, sem + 3, tr, near_col)
        finish_but_one(jnp.logical_or(is_diag, is_near), sem + 3, ured.at[app], 4 * COLS)

    def reduce_coarse(app):
        wait_bytes(ured.at[app], rsem.at[APP + 4 * app + 3])
        u = []
        for h in range(4):
            total = ured[app, h * COLS].astype(F32)
            for t in range(1, COLS):
                total = total + ured[app, h * COLS + t].astype(F32)
            u.append(total)
        return u

    def prolong(u, j):
        home = 1 + j // KR
        side = u[home - 1] * (1.0 - plus[j]) + u[home + 1] * plus[j]
        value = mm(jnp.concatenate(split(u[home]), axis=0), coef_ref[j, 0], NN)
        value = value + mm(jnp.concatenate(split(side), axis=0), coef_ref[j, 1], NN)
        return value[:VS] + value[VS:]

    def to_native(src, dst, sem):
        for t in OFFSETS:
            dy, dx = t
            q = lax.rem(odd * COLS + c + 4 * dy + dx, ROWS)
            tr = first_row + lax.div(q, COLS)
            tc = lax.rem(q, COLS)
            if t == (0, 0):
                either(is_diag, src.at[q], dst.at[r], sem, tr, tc)
            else:
                remote(src.at[q], dst.at[r], sem, tr, tc)
        finish_but_one(is_diag, sem, src, ROWS)

    lanes = lax.broadcasted_iota(jnp.int32, (VS, HALF), 1)
    vecs = lax.broadcasted_iota(jnp.int32, (VS, HALF), 0)

    def place(shift):
        return lanes == vecs + VS * shift

    own_place = place(lax.rem(r, 8))

    def as_row(v):
        return jnp.sum(jnp.where(own_place, v, 0.0), axis=0, keepdims=True)

    def as_column(row, mask):
        return jnp.sum(jnp.where(mask, row, 0.0), axis=1, keepdims=True)

    def s_block(j):
        return jnp.concatenate([scol[2 * j], scol[2 * j + 1]], axis=1) * PRESCALE

    def d_block(j):
        return jnp.concatenate([ecol[2 * j], ecol[2 * j + 1]], axis=1) - SHIFT

    def row_sum(v):
        return jnp.sum(v, axis=1, keepdims=True)

    def left_part():
        for i in range(KR):
            for n in range(2):
                cit[i, n] = ci[i, n].T
        for i in range(KR):
            flag = map_ref[1, r * KR + i] == r_next
            row = jnp.where(flag, 8, 0)
            for b in range(4):
                value = mm(cit[i, 0], kbuf[4 + b], NN) + mm(cit[i, 1], kbuf[row + b], NN)
                lbuf[b, pl.ds(i * BANDS, BANDS), :] = value.astype(BF16)

    def tile_piece(j):
        home = 1 + j // KR
        flag = map_ref[1, c * FINE + j] == lax.rem(c * 2 + j // KR + 1, ROWS)
        other = jnp.where(flag, home + 1, home - 1)
        for m in range(KR):
            rows = pl.ds(m * BANDS, BANDS)
            value = mm(lbuf[home, rows], coef_ref[j, 0], NN) + mm(lbuf[other, rows], coef_ref[j, 1], NN)
            tbuf[j, rows, :] = value.astype(BF16)
        pltpu.make_async_copy(
            tbuf.at[j], tile_ref.at[:, pl.ds(j * BANDS, BANDS)], tsem.at[j]
        ).start()

    wait_bytes(scol, rsem.at[S])
    restrict([s_block(j) for j in range(FINE)], 0)
    bulk_direct(1)
    coarse_apply(0)
    bulk_second()
    u = reduce_coarse(0)
    wait_bytes(ecol, rsem.at[E])
    parts = []
    ss = sg = gg = jnp.zeros((VS, 1), F32)
    for j in range(FINE):
        s_j = s_block(j)
        g_j = prolong(u, j) + d_block(j) * s_j
        gcol[j] = g_j
        parts.append(g_j)
        ss = ss + row_sum(s_j * s_j)
        sg = sg + row_sum(s_j * g_j)
        gg = gg + row_sum(g_j * g_j)

    restrict(parts, 1)
    for n, v in enumerate((ss, sg, gg)):
        zs_send[n] = as_row(v)
    local(zs_send, zs_recv.at[c], ZS)
    for t in range(1, COLS):
        remote(zs_send, zs_recv.at[c], ZS, r, lax.rem(c + t, COLS))
    finish_plain(ZS, zs_recv.at[pl.ds(0, COLS - 1)])
    bulk_siblings()
    bulk_wait()
    left_part()
    wait_bytes(zs_recv, rsem.at[ZS])
    mean = zs_recv[0]
    for t in range(1, COLS):
        mean = mean + zs_recv[t]
    mean = mean / ORDER
    ss, sg, gg = (as_column(mean[n], own_place) for n in range(3))
    var = ss + EPS * PRESCALE * PRESCALE
    scale = jnp.sqrt(var)
    alpha_one = (sg + SHIFT * ss) / var
    mix = SHIFT - alpha_one
    remain_sq = (gg + 2.0 * mix * sg + mix * mix * ss) / var
    beta = jnp.sqrt(jnp.maximum(remain_sq, 0.0) + EPS)
    inv = 1.0 / (scale * beta)
    ab_send[0] = as_row(alpha_one)
    ab_send[1] = as_row(beta)
    for j in range(FINE):
        sec = (gcol[j] + mix * s_block(j)) * inv
        for h in range(2):
            sec_send[2 * j + h] = sec[:, h * HALF:(h + 1) * HALF]
    to_native(sec_send, sec_nat, SEC)
    for t in OFFSETS:
        if t == (0, 0):
            local(ab_send, ab_recv.at[r], AB)
        else:
            remote(ab_send, ab_recv.at[r], AB, plane_row(t), c)
    finish_plain(AB, ab_recv.at[pl.ds(0, ROWS - 1)])
    coarse_apply(1)
    for j in range(4):
        tile_piece(j)

    u = reduce_coarse(1)
    over = beta / scale
    dot = jnp.zeros((VS, 1), F32)
    for j in range(FINE):
        s_j = s_block(j)
        g_j = gcol[j]
        h_j = prolong(u, j) + d_block(j) * g_j
        sec = jnp.concatenate([sec_send[2 * j], sec_send[2 * j + 1]], axis=1)
        shifted = (h_j + mix * g_j) * inv + SHIFT * sec - over * s_j
        dot = dot + row_sum(sec * shifted)
        for h in range(2):
            sh_send[2 * j + h] = shifted[:, h * HALF:(h + 1) * HALF]
    dot_send[...] = as_row(dot)
    for tz in AROUND:
        for t in OFFSETS:
            if t == (0, 0) and tz == 0:
                local(dot_send, dot_recv.at[c * ROWS + r], DOT)
            else:
                remote(dot_send, dot_recv.at[c * ROWS + r], DOT, plane_row(t), lax.rem(c + tz, COLS))
    finish_plain(DOT, dot_recv.at[pl.ds(0, ROWS * COLS - 1)])
    to_native(sh_send, sh_nat, SH)
    for j in range(4, FINE):
        tile_piece(j)

    wait_bytes(sec_nat, rsem.at[SEC])
    second_ref[...] = sec_nat[...].reshape(NVEC, HALF)
    wait_bytes(ab_recv, rsem.at[AB])
    wait_bytes(dot_recv, rsem.at[DOT])
    wait_bytes(sh_nat, rsem.at[SH])
    total = dot_recv[pl.ds(0, ROWS)]
    for t in range(1, COLS):
        total = total + dot_recv[pl.ds(t * ROWS, ROWS)]
    alpha_two = total / ORDER

    for i in range(ROWS):
        column = as_column(alpha_two[i], place(i % 8))
        resid_ref[pl.ds(i * VS, VS), :] = sh_nat[i] - column * sec_nat[i]
    rows = []
    for get in (lambda i: ab_recv[i, 0], lambda i: ab_recv[i, 1], lambda i: alpha_two[i]):
        halves = []
        for h in range(2):
            value = get(8 * h)
            for i in range(1, 8):
                value = value + get(8 * h + i)
            halves.append(value)
        rows.append(jnp.concatenate(halves, axis=1))
    coeffs_ref[...] = jnp.concatenate(rows, axis=0)

    for j in range(FINE):
        pltpu.make_async_copy(
            tbuf.at[j], tile_ref.at[:, pl.ds(j * BANDS, BANDS)], tsem.at[j]
        ).wait()
    for run in finish:
        run()


def per_device(coarse_kernel, interp_coef, interp_map, energy, start_vectors):
    vmem = pl.BlockSpec(memory_space=pltpu.VMEM)
    anywhere = pl.BlockSpec(memory_space=pl.ANY)
    nsem = 12 + 8
    return pl.pallas_call(
        kernel,
        out_shape=(
            jax.ShapeDtypeStruct((NVEC, HALF), F32),
            jax.ShapeDtypeStruct((NVEC, HALF), F32),
            jax.ShapeDtypeStruct((3, NVEC), F32),
            jax.ShapeDtypeStruct((KR * BANDS, FINE * BANDS), BF16),
        ),
        in_specs=[pl.BlockSpec(memory_space=pltpu.SMEM), anywhere, anywhere, anywhere, anywhere],
        out_specs=(vmem, vmem, vmem, anywhere),
        scratch_shapes=[
            pltpu.VMEM((1, 2, BANDS, BANDS), BF16),
            pltpu.VMEM((FINE, 2, BANDS, BANDS), BF16),
            pltpu.VMEM((1, HALF), F32),
            pltpu.VMEM((NVEC, HALF), F32),
            pltpu.VMEM((16, VS, HALF), F32),
            pltpu.VMEM((16, 1, HALF), F32),
            pltpu.VMEM((FINE, VS, BANDS), F32),
            pltpu.VMEM((12, BANDS, BANDS), BF16),
            pltpu.VMEM((KR, 2, BANDS, BANDS), BF16),
            pltpu.VMEM((KR, 2, BANDS, BANDS), BF16),
            pltpu.VMEM((4, KR * BANDS, BANDS), BF16),
            pltpu.VMEM((FINE, KR * BANDS, BANDS), BF16),
            pltpu.VMEM((2, VS, 2 * BANDS), BF16),
            pltpu.VMEM((2, 2, VS, BANDS), BF16),
            pltpu.VMEM((2, ROWS, VS, 2 * BANDS), BF16),
            pltpu.VMEM((2, ROWS, VS, BANDS), BF16),
            pltpu.VMEM((2, ROWS, VS, BANDS), BF16),
            pltpu.VMEM((2, ROWS, VS, BANDS), BF16),
            pltpu.VMEM((2, 4 * COLS, VS, BANDS), BF16),
            pltpu.VMEM((3, 1, HALF), F32),
            pltpu.VMEM((COLS, 3, 1, HALF), F32),
            pltpu.VMEM((2, 1, HALF), F32),
            pltpu.VMEM((ROWS, 2, 1, HALF), F32),
            pltpu.VMEM((16, VS, HALF), F32),
            pltpu.VMEM((16, VS, HALF), F32),
            pltpu.VMEM((16, VS, HALF), F32),
            pltpu.VMEM((16, VS, HALF), F32),
            pltpu.VMEM((1, HALF), F32),
            pltpu.VMEM((COLS * ROWS, 1, HALF), F32),
            pltpu.SemaphoreType.DMA((nsem,)),
            pltpu.SemaphoreType.DMA((nsem,)),
            pltpu.SemaphoreType.DMA((FINE,)),
            pltpu.SemaphoreType.DMA((4,)),
        ],
        compiler_params=pltpu.CompilerParams(
            has_side_effects=True, collective_id=0, vmem_limit_bytes=60 * 1024 * 1024
        ),
    )(interp_map.T, coarse_kernel, interp_coef, energy.reshape(1, HALF), start_vectors)


def solution(mesh):
    return jax.shard_map(
        per_device,
        mesh=mesh,
        in_specs=(
            P("row", "col", None, None),
            P("col", None, None, None),
            P(),
            P(("row", "col")),
            P(None, ("row", "col")),
        ),
        out_specs=(P(None, ("row", "col")), P(None, ("row", "col")), P(), P("row", "col")),
        check_vma=False,
    )
```

```python
import jax
import jax.numpy as jnp
from jax import lax
from jax.experimental import pallas as pl
from jax.experimental.pallas import tpu as pltpu
from jax.sharding import PartitionSpec as P

ROWS = 16
COLS = 8
BANDS = 256
NVEC = 256
FINE = 8
KR = 4
VS = NVEC // ROWS
HALF = 128
ORDER = 16384
EPS = 1e-06
PRESCALE = 0.125
SHIFT = 2.0

F32 = jnp.float32
BF16 = jnp.bfloat16
MESH = pl.DeviceIdType.MESH

NT = (((1,), (1,)), ((), ()))
NN = (((1,), (0,)), ((), ()))

OFFSETS = sorted(
    ((dy, dx) for dy in range(4) for dx in range(4)),
    key=lambda t: -(min(t[0], 4 - t[0]) + min(t[1], 4 - t[1])),
)
AROUND = (4, 2, 6, 3, 5, 1, 7, 0)


def mm(a, b, dims):
    return lax.dot_general(a, b, dims, preferred_element_type=F32)


def wait_bytes(ref, sem):
    pltpu.make_async_copy(ref, ref, sem).wait()


def kernel(
    map_hbm, kc_hbm, coef_hbm, e_hbm, s_hbm,
    second_ref, resid_ref, coeffs_ref, tile_ref,
    map_ref, kc_ref, coef_ref, e_ref, s_ref,
    scol, ecol, gcol, kbuf, cj, ci, cit, lbuf,
    wsend, wside, wfull, wlow, whigh, usend, ured,
    zs_send, zs_recv, ab_send, ab_recv, y_send, y_nat, z_send, z_nat, dot_send, dot_recv,
    ssem, rsem, lsem,
):
    r = lax.axis_index("row")
    c = lax.axis_index("col")
    z = lax.div(c, 2)
    k = lax.rem(c, 2)
    x = lax.rem(r, 4)
    y = lax.div(r, 4)
    odd = lax.rem(r, 2)
    c_prev = lax.rem(c + COLS - 1, COLS)
    c_next = lax.rem(c + 1, COLS)
    diag_col = lax.div(r, 2)
    near_col = lax.rem(diag_col + COLS - 1 + 2 * odd, COLS)
    is_diag = c == diag_col
    is_near = c == near_col
    first_row = 2 * c
    sibling = 2 * z + (1 - k)
    finish = []

    loads = []
    for n, (src, dst) in enumerate(((s_hbm, s_ref), (e_hbm, e_ref), (kc_hbm, kc_ref), (coef_hbm, coef_ref), (map_hbm, map_ref))):
        loads.append(pltpu.make_async_copy(src, dst, lsem.at[n]))
        loads[-1].start()

    barrier = pltpu.get_barrier_semaphore()

    def greet(tr, tc):
        pl.semaphore_signal(barrier, inc=1, device_id=(tr, tc), device_id_type=MESH)

    def plane_row(t):
        dy, dx = t
        return 4 * lax.rem(y + dy, 4) + lax.rem(x + dx, 4)

    for tz in AROUND:
        for t in OFFSETS:
            if tz or t != (0, 0):
                greet(plane_row(t), lax.rem(c + tz, COLS))
    pl.semaphore_wait(barrier, ROWS * COLS - 1)

    def remote(src, dst, sem, tr, tc, out=None):
        pltpu.make_async_remote_copy(
            src_ref=src, dst_ref=dst, recv_sem=rsem.at[sem],
            send_sem=ssem.at[sem if out is None else out],
            device_id=(tr, tc), device_id_type=MESH,
        ).start()

    def local(src, dst, sem):
        pltpu.make_async_copy(src, dst, rsem.at[sem]).start()

    def either(here, src, dst, sem, tr, tc):
        @pl.when(here)
        def _():
            local(src, dst, sem)

        @pl.when(jnp.logical_not(here))
        def _():
            remote(src, dst, sem, tr, tc)

    def finish_plain(sem, buf):
        finish.append(lambda: wait_bytes(buf, ssem.at[sem]))

    def finish_but_one(here, sem, buf, count):
        def run():
            @pl.when(here)
            def _():
                wait_bytes(buf.at[pl.ds(0, count - 1)], ssem.at[sem])

            @pl.when(jnp.logical_not(here))
            def _():
                wait_bytes(buf.at[pl.ds(0, count)], ssem.at[sem])

        finish.append(run)

    S, E, K1, K2, CB, AB, YN, ZN, DOT, ZS = range(10)
    C1, C3, APP = 10, 14, 18

    loads[0].wait()
    loads[1].wait()
    for t in OFFSETS:
        tr = plane_row(t)
        src = s_ref.at[pl.ds(pl.multiple_of(tr * VS, VS), VS), :]
        dst = scol.at[odd * COLS + c]
        if t == (0, 0):
            either(is_diag, src, dst, S, tr, diag_col)
        else:
            remote(src, dst, S, tr, diag_col)
    finish_but_one(is_diag, S, scol, ROWS)
    for t in OFFSETS:
        tr = plane_row(t)
        dst = ecol.at[odd * COLS + c]
        if t == (0, 0):
            either(is_diag, e_ref, dst, E, tr, diag_col)
        else:
            remote(e_ref, dst, E, tr, diag_col)
    finish_but_one(is_diag, E, ecol, ROWS)
    loads[2].wait()
    loads[3].wait()
    loads[4].wait()

    delta = lax.rem(y - z + 4, 4)
    mine = lax.rem(x, 2) * KR + delta
    home_core = lax.div(x, 2)
    at_source = delta == 0
    serves = k == home_core
    is_home = jnp.logical_and(at_source, serves)
    r_next = lax.rem(r + 1, ROWS)
    r_prev = lax.rem(r + ROWS - 1, ROWS)
    pair = pl.ds(2 * k, 2)
    piece = [lax.rem(delta + t, 4) for t in range(4)]
    holds = [lax.div(p, 2) == k for p in piece]

    def ring_col(t, core):
        return 2 * lax.rem(z + t, 4) + core

    def bulk_first():
        remote(kc_ref.at[0], kbuf.at[pl.ds(1, 2)], K1, r_next, c)
        remote(kc_ref.at[0], kbuf.at[pl.ds(9, 2)], K1, r_prev, c)

        @pl.when(serves)
        def _():
            for t in (1, 3):
                remote(coef_ref.at[mine], cj.at[t], C1 + t, r, ring_col(t, lax.div(delta, 2)), C1)

    def bulk_second():
        for t in (1, 3):
            @pl.when(holds[t])
            def _(t=t):
                wait_bytes(cj.at[t], rsem.at[C1 + t])
                n = t // 2
                remote(cj.at[t, n], cj.at[2, n], C1 + 2, r, ring_col(t, k), C1 + t)

        wait_bytes(kbuf.at[pl.ds(0, 4)], rsem.at[K1])
        for slot in range(3):
            remote(kbuf.at[4 * slot + 1], kbuf.at[4 * slot + 3], K2, r, c_prev)
            remote(kbuf.at[4 * slot + 2], kbuf.at[4 * slot], K2, r, c_next)

    def bulk_third():
        @pl.when(holds[2])
        def _():
            wait_bytes(cj.at[2], rsem.at[C1 + 2])

        for t in (1, 2, 3):
            @pl.when(jnp.logical_and(holds[t], piece[t] != 0))
            def _(t=t):
                remote(cj.at[t], ci.at[piece[t]], C3, 4 * lax.rem(z + 4 - t, 4) + x, c, C3 + t)

            @pl.when(jnp.logical_and(holds[t], piece[t] == 0))
            def _(t=t):
                local(cj.at[t], ci.at[0], C3)

    def bulk_siblings():
        @pl.when(jnp.logical_not(at_source))
        def _():
            wait_bytes(ci.at[pl.ds(0, 2)], rsem.at[C3])
            remote(ci.at[pair], ci.at[pair], CB, r, sibling)

        @pl.when(is_home)
        def _():
            src = coef_ref.at[pl.ds(odd * KR, KR)]
            local(src, ci, C1)
            remote(src, ci, CB, r, sibling)

    def bulk_wait():
        @pl.when(is_home)
        def _():
            wait_bytes(ci, rsem.at[C1])

        @pl.when(jnp.logical_not(at_source))
        def _():
            wait_bytes(ci.at[pl.ds(0, 2)], rsem.at[CB])

        @pl.when(jnp.logical_and(at_source, k != home_core))
        def _():
            wait_bytes(ci, rsem.at[CB])

        wait_bytes(kbuf.at[pl.ds(0, 6)], rsem.at[K2])

    def bulk_finish():
        wait_bytes(kbuf.at[pl.ds(0, 4)], ssem.at[K1])
        wait_bytes(kbuf.at[pl.ds(0, 6)], ssem.at[K2])

        @pl.when(serves)
        def _():
            wait_bytes(ci.at[pl.ds(0, 2)], ssem.at[C1])

        for t in (1, 3):
            @pl.when(holds[t])
            def _(t=t):
                wait_bytes(kbuf.at[0], ssem.at[C1 + t])

        for t in (1, 2, 3):
            @pl.when(jnp.logical_and(holds[t], piece[t] != 0))
            def _(t=t):
                wait_bytes(ci.at[0], ssem.at[C3 + t])

        @pl.when(jnp.logical_not(at_source))
        def _():
            wait_bytes(ci.at[pl.ds(0, 2)], ssem.at[CB])

        @pl.when(is_home)
        def _():
            wait_bytes(ci, ssem.at[CB])

    finish.append(bulk_finish)
    bulk_first()
    for b in range(2):
        kbuf[5 + b] = kc_ref[0, b]

    plus = []
    for j in range(FINE):
        home = c * 2 + j // KR
        flag = map_ref[1, c * FINE + j] == lax.rem(home + 1, ROWS)
        plus.append(flag.astype(F32))

    def split(v):
        high = v.astype(BF16)
        return high, (v - high.astype(F32)).astype(BF16)

    def restrict(parts, app):
        acc = [jnp.zeros((VS, BANDS), F32) for _ in range(4)]
        for j in range(FINE):
            home = 1 + j // KR
            high, low = split(parts[j])
            both = jnp.concatenate([high, low], axis=0)
            up = (both.astype(F32) * plus[j]).astype(BF16)
            down = both - up
            own = mm(both, coef_ref[j, 0], NT)
            side = mm(jnp.concatenate([down, up], axis=0), coef_ref[j, 1], NT)
            acc[home] = acc[home] + own[:VS] + own[VS:]
            acc[home - 1] = acc[home - 1] + side[:VS] + side[VS:2 * VS]
            acc[home + 1] = acc[home + 1] + side[2 * VS:3 * VS] + side[3 * VS:]
        wsend[app] = jnp.concatenate([acc[1], acc[2]], axis=1).astype(BF16)
        wside[app, 0] = acc[0].astype(BF16)
        wside[app, 1] = acc[3].astype(BF16)
        sem = APP + 4 * app
        for t in OFFSETS:
            tr = plane_row(t)
            remote(wside.at[app, 0], whigh.at[app, r], sem, tr, c_prev)
            remote(wside.at[app, 1], wlow.at[app, r], sem + 1, tr, c_next)
            if t == (0, 0):
                local(wsend.at[app], wfull.at[app, r], sem + 2)
            else:
                remote(wsend.at[app], wfull.at[app, r], sem + 2, tr, c)
        finish_plain(sem, whigh.at[app])
        finish_plain(sem + 1, wlow.at[app])
        finish_plain(sem + 2, wfull.at[app, pl.ds(0, ROWS - 1)])

    def coarse_apply(app):
        sem = APP + 4 * app
        wait_bytes(wfull.at[app], rsem.at[sem + 2])
        wait_bytes(whigh.at[app], rsem.at[sem])
        wait_bytes(wlow.at[app], rsem.at[sem + 1])
        full = wfull[app].reshape(NVEC, 2 * BANDS)
        part = mm(full[:, :BANDS], kc_ref[0, 0], NT) + mm(full[:, BANDS:], kc_ref[0, 1], NT)
        part = part + mm(wlow[app].reshape(NVEC, BANDS), kc_ref[0, 0], NT)
        part = part + mm(whigh[app].reshape(NVEC, BANDS), kc_ref[0, 1], NT)
        usend[app] = part.astype(BF16).reshape(ROWS, VS, BANDS)
        for t in OFFSETS:
            tr = plane_row(t)
            src = usend.at[app, tr]
            own = ured.at[app, (1 + odd) * COLS + c]
            near = ured.at[app, 3 * (1 - odd) * COLS + c]
            if t == (0, 0):
                either(is_diag, src, own, sem + 3, tr, diag_col)
                either(is_near, src, near, sem + 3, tr, near_col)
            else:
                remote(src, own, sem + 3, tr, diag_col)
                remote(src, near, sem + 3, tr, near_col)
        finish_but_one(jnp.logical_or(is_diag, is_near), sem + 3, ured.at[app], 4 * COLS)

    def reduce_coarse(app):
        wait_bytes(ured.at[app], rsem.at[APP + 4 * app + 3])
        u = []
        for h in range(4):
            total = ured[app, h * COLS].astype(F32)
            for t in range(1, COLS):
                total = total + ured[app, h * COLS + t].astype(F32)
            u.append(total)
        return u

    def prolong(u, j):
        home = 1 + j // KR
        side = u[home - 1] * (1.0 - plus[j]) + u[home + 1] * plus[j]
        value = mm(jnp.concatenate(split(u[home]), axis=0), coef_ref[j, 0], NN)
        value = value + mm(jnp.concatenate(split(side), axis=0), coef_ref[j, 1], NN)
        return value[:VS] + value[VS:]

    def to_native(src, dst, sem):
        for t in OFFSETS:
            dy, dx = t
            q = lax.rem(odd * COLS + c + 4 * dy + dx, ROWS)
            tr = first_row + lax.div(q, COLS)
            tc = lax.rem(q, COLS)
            if t == (0, 0):
                either(is_diag, src.at[q], dst.at[r], sem, tr, tc)
            else:
                remote(src.at[q], dst.at[r], sem, tr, tc)
        finish_but_one(is_diag, sem, src, ROWS)

    lanes = lax.broadcasted_iota(jnp.int32, (VS, HALF), 1)
    vecs = lax.broadcasted_iota(jnp.int32, (VS, HALF), 0)

    def place(shift):
        return lanes == vecs + VS * shift

    own_place = place(lax.rem(r, 8))

    def as_row(v):
        return jnp.sum(jnp.where(own_place, v, 0.0), axis=0, keepdims=True)

    def as_column(row, mask):
        return jnp.sum(jnp.where(mask, row, 0.0), axis=1, keepdims=True)

    def s_block(j):
        return jnp.concatenate([scol[2 * j], scol[2 * j + 1]], axis=1) * PRESCALE

    def d_block(j):
        return jnp.concatenate([ecol[2 * j], ecol[2 * j + 1]], axis=1) - SHIFT

    def keep(buf, j, v):
        for h in range(2):
            buf[2 * j + h] = v[:, h * HALF:(h + 1) * HALF].astype(BF16)

    def row_sum(v):
        return jnp.sum(v, axis=1, keepdims=True)

    def left_part():
        for i in range(KR):
            for n in range(2):
                cit[i, n] = ci[i, n].T
        for i in range(KR):
            flag = map_ref[1, r * KR + i] == r_next
            row = jnp.where(flag, 8, 0)
            for b in range(4):
                value = mm(cit[i, 0], kbuf[4 + b], NN) + mm(cit[i, 1], kbuf[row + b], NN)
                lbuf[b, pl.ds(i * BANDS, BANDS), :] = value.astype(BF16)

    def tile_piece(j):
        home = 1 + j // KR
        flag = map_ref[1, c * FINE + j] == lax.rem(c * 2 + j // KR + 1, ROWS)
        other = jnp.where(flag, home + 1, home - 1)
        for m in range(KR):
            rows = pl.ds(m * BANDS, BANDS)
            value = mm(lbuf[home, rows], coef_ref[j, 0], NN) + mm(lbuf[other, rows], coef_ref[j, 1], NN)
            tile_ref[rows, pl.ds(j * BANDS, BANDS)] = value.astype(BF16)

    wait_bytes(scol, rsem.at[S])
    restrict([s_block(j) for j in range(FINE)], 0)
    bulk_second()
    coarse_apply(0)
    bulk_third()
    u = reduce_coarse(0)
    wait_bytes(ecol, rsem.at[E])
    parts = []
    ss = sg = gg = jnp.zeros((VS, 1), F32)
    for j in range(FINE):
        s_j = s_block(j)
        y_j = prolong(u, j)
        g_j = y_j + d_block(j) * s_j
        gcol[j] = g_j
        parts.append(g_j)
        keep(y_send, j, y_j)
        ss = ss + row_sum(s_j * s_j)
        sg = sg + row_sum(s_j * g_j)
        gg = gg + row_sum(g_j * g_j)

    restrict(parts, 1)
    for n, v in enumerate((ss, sg, gg)):
        zs_send[n] = as_row(v)
    local(zs_send, zs_recv.at[c], ZS)
    for t in range(1, COLS):
        remote(zs_send, zs_recv.at[c], ZS, r, lax.rem(c + t, COLS))
    finish_plain(ZS, zs_recv.at[pl.ds(0, COLS - 1)])
    wait_bytes(zs_recv, rsem.at[ZS])
    mean = zs_recv[0]
    for t in range(1, COLS):
        mean = mean + zs_recv[t]
    mean = mean / ORDER
    ss, sg, gg = (as_column(mean[n], own_place) for n in range(3))
    var = ss + EPS * PRESCALE * PRESCALE
    scale = jnp.sqrt(var)
    alpha_one = (sg + SHIFT * ss) / var
    mix = SHIFT - alpha_one
    remain_sq = (gg + 2.0 * mix * sg + mix * mix * ss) / var
    beta = jnp.sqrt(jnp.maximum(remain_sq, 0.0) + EPS)
    inv = 1.0 / (scale * beta)
    over = beta / scale
    for n, v in enumerate((alpha_one, beta, inv, over)):
        ab_send[n] = as_row(v)
    coarse_apply(1)
    for t in OFFSETS:
        if t == (0, 0):
            local(ab_send, ab_recv.at[r], AB)
        else:
            remote(ab_send, ab_recv.at[r], AB, plane_row(t), c)
    finish_plain(AB, ab_recv.at[pl.ds(0, ROWS - 1)])
    to_native(y_send, y_nat, YN)
    bulk_siblings()
    bulk_wait()
    left_part()

    u = reduce_coarse(1)
    dot = jnp.zeros((VS, 1), F32)
    for j in range(FINE):
        s_j = s_block(j)
        g_j = gcol[j]
        z_j = prolong(u, j)
        h_j = z_j + d_block(j) * g_j
        sec = (g_j + mix * s_j) * inv
        shifted = (h_j + mix * g_j) * inv + SHIFT * sec - over * s_j
        dot = dot + row_sum(sec * shifted)
        keep(z_send, j, z_j)
    dot_send[...] = as_row(dot)
    for tz in AROUND:
        for t in OFFSETS:
            if t == (0, 0) and tz == 0:
                local(dot_send, dot_recv.at[c * ROWS + r], DOT)
            else:
                remote(dot_send, dot_recv.at[c * ROWS + r], DOT, plane_row(t), lax.rem(c + tz, COLS))
    finish_plain(DOT, dot_recv.at[pl.ds(0, ROWS * COLS - 1)])
    to_native(z_send, z_nat, ZN)
    for j in range(FINE):
        tile_piece(j)

    wait_bytes(y_nat, rsem.at[YN])
    wait_bytes(ab_recv, rsem.at[AB])
    diag = e_ref[...] - SHIFT
    for i in range(ROWS):
        rows = pl.ds(i * VS, VS)
        mask = place(i % 8)
        first = s_ref[rows, :] * PRESCALE
        image = y_nat[i].astype(F32) + diag * first
        mix_i = SHIFT - as_column(ab_recv[i, 0], mask)
        inv_i = as_column(ab_recv[i, 2], mask)
        over_i = as_column(ab_recv[i, 3], mask)
        sec = (image + mix_i * first) * inv_i
        second_ref[rows, :] = sec
        resid_ref[rows, :] = (diag * image + mix_i * image) * inv_i + SHIFT * sec - over_i * first
    wait_bytes(dot_recv, rsem.at[DOT])
    total = dot_recv[pl.ds(0, ROWS)]
    for t in range(1, COLS):
        total = total + dot_recv[pl.ds(t * ROWS, ROWS)]
    alpha_two = total / ORDER
    lines = []
    for get in (lambda i: ab_recv[i, 0], lambda i: ab_recv[i, 1], lambda i: alpha_two[i]):
        halves = []
        for h in range(2):
            value = get(8 * h)
            for i in range(1, 8):
                value = value + get(8 * h + i)
            halves.append(value)
        lines.append(jnp.concatenate(halves, axis=1))
    coeffs_ref[...] = jnp.concatenate(lines, axis=0)
    wait_bytes(z_nat, rsem.at[ZN])
    for i in range(ROWS):
        rows = pl.ds(i * VS, VS)
        mask = place(i % 8)
        column = as_column(alpha_two[i], mask)
        inv_i = as_column(ab_recv[i, 2], mask)
        resid_ref[rows, :] = resid_ref[rows, :] + z_nat[i].astype(F32) * inv_i - column * second_ref[rows, :]

    for run in finish:
        run()


def write_out(*refs):
    copies = [pltpu.make_async_copy(refs[n], refs[4 + n], refs[8].at[n]) for n in range(4)]
    for copy in copies:
        copy.start()
    for copy in copies:
        copy.wait()


def per_device(coarse_kernel, interp_coef, interp_map, energy, start_vectors):
    vmem = pl.BlockSpec(memory_space=pltpu.VMEM)
    hbm = pl.BlockSpec(memory_space=pltpu.HBM)
    nsem = 18 + 8
    shapes = (
        jax.ShapeDtypeStruct((NVEC, HALF), F32),
        jax.ShapeDtypeStruct((NVEC, HALF), F32),
        jax.ShapeDtypeStruct((3, NVEC), F32),
        jax.ShapeDtypeStruct((KR * BANDS, FINE * BANDS), BF16),
    )
    operands = (interp_map.T, coarse_kernel, interp_coef, energy.reshape(1, HALF), start_vectors)
    results = pl.pallas_call(
        kernel,
        out_shape=shapes,
        in_specs=[hbm] * 5,
        out_specs=(vmem, vmem, vmem, vmem),
        scratch_shapes=[
            pltpu.SMEM((2, COLS * FINE), jnp.int32),
            pltpu.VMEM((1, 2, BANDS, BANDS), BF16),
            pltpu.VMEM((FINE, 2, BANDS, BANDS), BF16),
            pltpu.VMEM((1, HALF), F32),
            pltpu.VMEM((NVEC, HALF), F32),
            pltpu.VMEM((16, VS, HALF), F32),
            pltpu.VMEM((16, 1, HALF), F32),
            pltpu.VMEM((FINE, VS, BANDS), F32),
            pltpu.VMEM((12, BANDS, BANDS), BF16),
            pltpu.VMEM((4, 2, BANDS, BANDS), BF16),
            pltpu.VMEM((KR, 2, BANDS, BANDS), BF16),
            pltpu.VMEM((KR, 2, BANDS, BANDS), BF16),
            pltpu.VMEM((4, KR * BANDS, BANDS), BF16),
            pltpu.VMEM((2, VS, 2 * BANDS), BF16),
            pltpu.VMEM((2, 2, VS, BANDS), BF16),
            pltpu.VMEM((2, ROWS, VS, 2 * BANDS), BF16),
            pltpu.VMEM((2, ROWS, VS, BANDS), BF16),
            pltpu.VMEM((2, ROWS, VS, BANDS), BF16),
            pltpu.VMEM((2, ROWS, VS, BANDS), BF16),
            pltpu.VMEM((2, 4 * COLS, VS, BANDS), BF16),
            pltpu.VMEM((3, 1, HALF), F32),
            pltpu.VMEM((COLS, 3, 1, HALF), F32),
            pltpu.VMEM((4, 1, HALF), F32),
            pltpu.VMEM((ROWS, 4, 1, HALF), F32),
            pltpu.VMEM((16, VS, HALF), BF16),
            pltpu.VMEM((16, VS, HALF), BF16),
            pltpu.VMEM((16, VS, HALF), BF16),
            pltpu.VMEM((16, VS, HALF), BF16),
            pltpu.VMEM((1, HALF), F32),
            pltpu.VMEM((COLS * ROWS, 1, HALF), F32),
            pltpu.SemaphoreType.DMA((nsem,)),
            pltpu.SemaphoreType.DMA((nsem,)),
            pltpu.SemaphoreType.DMA((5,)),
        ],
        compiler_params=pltpu.CompilerParams(
            has_side_effects=True, collective_id=0, vmem_limit_bytes=40 * 1024 * 1024
        ),
    )(*(pltpu.with_memory_space_constraint(v, pltpu.HBM) for v in operands))
    return pl.pallas_call(
        write_out,
        out_shape=shapes,
        in_specs=[vmem] * 4,
        out_specs=(hbm,) * 4,
        scratch_shapes=[pltpu.SemaphoreType.DMA((4,))],
        compiler_params=pltpu.CompilerParams(vmem_limit_bytes=1024 * 1024),
    )(*results)


def solution(mesh):
    return jax.shard_map(
        per_device,
        mesh=mesh,
        in_specs=(
            P("row", "col", None, None),
            P("col", None, None, None),
            P(),
            P(("row", "col")),
            P(None, ("row", "col")),
        ),
        out_specs=(P(None, ("row", "col")), P(None, ("row", "col")), P(), P("row", "col")),
        check_vma=False,
    )
```

```python
import jax
import jax.numpy as jnp
from jax import lax
from jax.experimental import pallas as pl
from jax.experimental.pallas import tpu as pltpu
from jax.sharding import PartitionSpec as P

ROWS = 16
COLS = 8
BANDS = 256
NVEC = 256
FINE = 8
KR = 4
VS = NVEC // ROWS
HALF = 128
ORDER = 16384
EPS = 1e-06
PRESCALE = 0.125
SHIFT = 2.0

F32 = jnp.float32
BF16 = jnp.bfloat16
MESH = pl.DeviceIdType.MESH

NT = (((1,), (1,)), ((), ()))
NN = (((1,), (0,)), ((), ()))

OFFSETS = sorted(
    ((dy, dx) for dy in range(4) for dx in range(4)),
    key=lambda t: -(min(t[0], 4 - t[0]) + min(t[1], 4 - t[1])),
)
AROUND = (4, 2, 6, 3, 5, 1, 7, 0)


def mm(a, b, dims):
    return lax.dot_general(a, b, dims, preferred_element_type=F32)


def wait_bytes(ref, sem):
    pltpu.make_async_copy(ref, ref, sem).wait()


def kernel(
    map_hbm, kc_hbm, coef_hbm, e_hbm, s_hbm,
    second_ref, resid_ref, coeffs_ref, tile_ref,
    map_ref, kc_ref, coef_ref, e_ref, s_ref,
    scol, ecol, gcol, kbuf, cj, ci, cit, lbuf,
    wsend, wside, wfull, wlow, whigh, usend, ured,
    zs_send, zs_recv, ab_send, ab_recv, y_send, y_nat, z_send, z_nat, dot_send, dot_recv,
    ssem, rsem, lsem,
):
    r = lax.axis_index("row")
    c = lax.axis_index("col")
    z = lax.div(c, 2)
    k = lax.rem(c, 2)
    x = lax.rem(r, 4)
    y = lax.div(r, 4)
    odd = lax.rem(r, 2)
    c_prev = lax.rem(c + COLS - 1, COLS)
    c_next = lax.rem(c + 1, COLS)
    diag_col = lax.div(r, 2)
    near_col = lax.rem(diag_col + COLS - 1 + 2 * odd, COLS)
    is_diag = c == diag_col
    is_near = c == near_col
    first_row = 2 * c
    r_next = lax.rem(r + 1, ROWS)
    r_prev = lax.rem(r + ROWS - 1, ROWS)
    sibling = 2 * z + (1 - k)
    finish = []

    loads = []
    for n, (src, dst) in enumerate(((s_hbm, s_ref), (e_hbm, e_ref), (kc_hbm, kc_ref), (coef_hbm, coef_ref), (map_hbm, map_ref))):
        loads.append(pltpu.make_async_copy(src, dst, lsem.at[n]))
        loads[-1].start()

    barrier = pltpu.get_barrier_semaphore()

    def greet(tr, tc):
        pl.semaphore_signal(barrier, inc=1, device_id=(tr, tc), device_id_type=MESH)

    def plane_row(t):
        dy, dx = t
        return 4 * lax.rem(y + dy, 4) + lax.rem(x + dx, 4)

    for q in range(ROWS):
        tr, tc = first_row + q // COLS, q % COLS

        @pl.when(jnp.logical_not(jnp.logical_and(tr == r, tc == c)))
        def _(tr=tr, tc=tc):
            greet(tr, tc)

    for t in OFFSETS:
        greet(plane_row(t), c_prev)
        greet(plane_row(t), c_next)
    for t in range(2, COLS - 1):
        greet(r, lax.rem(c + t, COLS))
    greet(r_next, c)
    greet(r_prev, c)
    pl.semaphore_wait(barrier, 16 + 32 + 5 + 2 - is_diag.astype(jnp.int32))

    def remote(src, dst, sem, tr, tc, out=None):
        pltpu.make_async_remote_copy(
            src_ref=src, dst_ref=dst, recv_sem=rsem.at[sem],
            send_sem=ssem.at[sem if out is None else out],
            device_id=(tr, tc), device_id_type=MESH,
        ).start()

    def local(src, dst, sem):
        pltpu.make_async_copy(src, dst, rsem.at[sem]).start()

    def either(here, src, dst, sem, tr, tc):
        @pl.when(here)
        def _():
            local(src, dst, sem)

        @pl.when(jnp.logical_not(here))
        def _():
            remote(src, dst, sem, tr, tc)

    def finish_plain(sem, buf):
        finish.append(lambda: wait_bytes(buf, ssem.at[sem]))

    def finish_but_one(here, sem, buf, count):
        def run():
            @pl.when(here)
            def _():
                wait_bytes(buf.at[pl.ds(0, count - 1)], ssem.at[sem])

            @pl.when(jnp.logical_not(here))
            def _():
                wait_bytes(buf.at[pl.ds(0, count)], ssem.at[sem])

        finish.append(run)

    S, E, K2, CB, AB, YN, ZN, DOT, ZS = range(9)
    K1, C1, C3, APP = 9, 11, 15, 19

    loads[0].wait()
    loads[1].wait()
    for t in OFFSETS:
        tr = plane_row(t)
        src = s_ref.at[pl.ds(pl.multiple_of(tr * VS, VS), VS), :]
        dst = scol.at[odd * COLS + c]
        if t == (0, 0):
            either(is_diag, src, dst, S, tr, diag_col)
        else:
            remote(src, dst, S, tr, diag_col)
    finish_but_one(is_diag, S, scol, ROWS)
    for t in OFFSETS:
        tr = plane_row(t)
        dst = ecol.at[odd * COLS + c]
        if t == (0, 0):
            either(is_diag, e_ref, dst, E, tr, diag_col)
        else:
            remote(e_ref, dst, E, tr, diag_col)
    finish_but_one(is_diag, E, ecol, ROWS)
    loads[2].wait()
    loads[3].wait()
    loads[4].wait()

    delta = lax.rem(y - z + 4, 4)
    mine = lax.rem(x, 2) * KR + delta
    home_core = lax.div(x, 2)
    at_source = delta == 0
    serves = k == home_core
    is_home = jnp.logical_and(at_source, serves)
    pair = pl.ds(2 * k, 2)
    piece = [lax.rem(delta + t, 4) for t in range(4)]
    holds = [lax.div(p, 2) == k for p in piece]

    def ring_col(t, core):
        return 2 * lax.rem(z + t, 4) + core

    def row_blocks(b):
        remote(kc_ref.at[0, b], kbuf.at[1 + b], K1 + b, r_next, c)
        remote(kc_ref.at[0, b], kbuf.at[9 + b], K1 + b, r_prev, c)

    def column_blocks(b):
        wait_bytes(kbuf.at[pl.ds(0, 2)], rsem.at[K1 + b])
        for slot in range(3):
            if b == 0:
                remote(kbuf.at[4 * slot + 1], kbuf.at[4 * slot + 3], K2, r, c_prev)
            else:
                remote(kbuf.at[4 * slot + 2], kbuf.at[4 * slot], K2, r, c_next)

    def bulk_first():
        row_blocks(0)

        @pl.when(serves)
        def _():
            for t in (1, 3):
                remote(coef_ref.at[mine], cj.at[t], C1 + t, r, ring_col(t, lax.div(delta, 2)), C1)

    def bulk_second():
        for t in (1, 3):
            @pl.when(holds[t])
            def _(t=t):
                wait_bytes(cj.at[t], rsem.at[C1 + t])
                n = t // 2
                remote(cj.at[t, n], cj.at[2, n], C1 + 2, r, ring_col(t, k), C1 + t)

        column_blocks(0)

    def bulk_third():
        row_blocks(1)

        @pl.when(holds[2])
        def _():
            wait_bytes(cj.at[2], rsem.at[C1 + 2])

        for t in (1, 2, 3):
            @pl.when(jnp.logical_and(holds[t], lax.rem(piece[t], 2) == 1))
            def _(t=t):
                remote(cj.at[t], ci.at[piece[t]], C3, 4 * lax.rem(z + 4 - t, 4) + x, c, C3 + t)

            @pl.when(jnp.logical_and(holds[t], piece[t] == 0))
            def _(t=t):
                local(cj.at[t], ci.at[0], C3)

        far_piece(0)

    def far_piece(n):
        for t in (1, 2, 3):
            @pl.when(jnp.logical_and(holds[t], piece[t] == 2))
            def _(t=t):
                remote(cj.at[t, n], ci.at[2, n], C3, 4 * lax.rem(z + 4 - t, 4) + x, c, C3 + t)

    def bulk_siblings():
        @pl.when(jnp.logical_not(at_source))
        def _():
            wait_bytes(ci.at[pl.ds(0, 2)], rsem.at[C3])
            remote(ci.at[pair], ci.at[pair], CB, r, sibling)

        @pl.when(is_home)
        def _():
            src = coef_ref.at[pl.ds(odd * KR, KR)]
            local(src, ci, C1)
            remote(src, ci, CB, r, sibling)

    def bulk_wait():
        @pl.when(is_home)
        def _():
            wait_bytes(ci, rsem.at[C1])

        @pl.when(jnp.logical_not(at_source))
        def _():
            wait_bytes(ci.at[pl.ds(0, 2)], rsem.at[CB])

        @pl.when(jnp.logical_and(at_source, k != home_core))
        def _():
            wait_bytes(ci, rsem.at[CB])

        wait_bytes(kbuf.at[pl.ds(0, 6)], rsem.at[K2])

    def bulk_finish():
        wait_bytes(kbuf.at[pl.ds(0, 2)], ssem.at[K1])
        wait_bytes(kbuf.at[pl.ds(0, 2)], ssem.at[K1 + 1])
        wait_bytes(kbuf.at[pl.ds(0, 6)], ssem.at[K2])

        @pl.when(serves)
        def _():
            wait_bytes(ci.at[pl.ds(0, 2)], ssem.at[C1])

        for t in (1, 3):
            @pl.when(holds[t])
            def _(t=t):
                wait_bytes(kbuf.at[0], ssem.at[C1 + t])

        for t in (1, 2, 3):
            @pl.when(jnp.logical_and(holds[t], piece[t] != 0))
            def _(t=t):
                wait_bytes(ci.at[0], ssem.at[C3 + t])

        @pl.when(jnp.logical_not(at_source))
        def _():
            wait_bytes(ci.at[pl.ds(0, 2)], ssem.at[CB])

        @pl.when(is_home)
        def _():
            wait_bytes(ci, ssem.at[CB])

    finish.append(bulk_finish)
    bulk_first()
    for b in range(2):
        kbuf[5 + b] = kc_ref[0, b]

    plus = []
    for j in range(FINE):
        home = c * 2 + j // KR
        flag = map_ref[1, c * FINE + j] == lax.rem(home + 1, ROWS)
        plus.append(flag.astype(F32))

    def split(v):
        high = v.astype(BF16)
        return high, (v - high.astype(F32)).astype(BF16)

    def restrict(parts, app):
        acc = [None] * 4

        def add(h, v):
            acc[h] = v if acc[h] is None else acc[h] + v

        for j in range(FINE):
            home = 1 + j // KR
            both = jnp.concatenate(split(parts[j]), axis=0)
            add(home, mm(both, coef_ref[j, 0], NT))
            if j % KR == 0:
                add(home - 1, mm(both, coef_ref[j, 1], NT))
            elif j % KR == KR - 1:
                add(home + 1, mm(both, coef_ref[j, 1], NT))
            else:
                up = both * plus[j].astype(BF16)
                side = mm(jnp.concatenate([both - up, up], axis=0), coef_ref[j, 1], NT)
                add(home - 1, side[:2 * VS])
                add(home + 1, side[2 * VS:])
        acc = [v[:VS] + v[VS:] for v in acc]
        wsend[app] = jnp.concatenate([acc[1], acc[2]], axis=1).astype(BF16)
        wside[app, 0] = acc[0].astype(BF16)
        wside[app, 1] = acc[3].astype(BF16)
        sem = APP + 4 * app
        for t in OFFSETS:
            tr = plane_row(t)
            remote(wside.at[app, 0], whigh.at[app, r], sem, tr, c_prev)
            remote(wside.at[app, 1], wlow.at[app, r], sem + 1, tr, c_next)
            if t == (0, 0):
                local(wsend.at[app], wfull.at[app, r], sem + 2)
            else:
                remote(wsend.at[app], wfull.at[app, r], sem + 2, tr, c)
        finish_plain(sem, whigh.at[app])
        finish_plain(sem + 1, wlow.at[app])
        finish_plain(sem + 2, wfull.at[app, pl.ds(0, ROWS - 1)])

    def coarse_apply(app):
        sem = APP + 4 * app
        wait_bytes(wfull.at[app], rsem.at[sem + 2])
        wait_bytes(whigh.at[app], rsem.at[sem])
        wait_bytes(wlow.at[app], rsem.at[sem + 1])
        full = wfull[app].reshape(NVEC, 2 * BANDS)
        part = mm(full[:, :BANDS], kc_ref[0, 0], NT) + mm(full[:, BANDS:], kc_ref[0, 1], NT)
        part = part + mm(wlow[app].reshape(NVEC, BANDS), kc_ref[0, 0], NT)
        part = part + mm(whigh[app].reshape(NVEC, BANDS), kc_ref[0, 1], NT)
        usend[app] = part.astype(BF16).reshape(ROWS, VS, BANDS)
        for t in OFFSETS:
            tr = plane_row(t)
            src = usend.at[app, tr]
            own = ured.at[app, (1 + odd) * COLS + c]
            near = ured.at[app, 3 * (1 - odd) * COLS + c]
            if t == (0, 0):
                either(is_diag, src, own, sem + 3, tr, diag_col)
                either(is_near, src, near, sem + 3, tr, near_col)
            else:
                remote(src, own, sem + 3, tr, diag_col)
                remote(src, near, sem + 3, tr, near_col)
        finish_but_one(jnp.logical_or(is_diag, is_near), sem + 3, ured.at[app], 4 * COLS)

    def reduce_coarse(app):
        wait_bytes(ured.at[app], rsem.at[APP + 4 * app + 3])
        u = []
        for h in range(4):
            total = ured[app, h * COLS].astype(F32)
            for t in range(1, COLS):
                total = total + ured[app, h * COLS + t].astype(F32)
            u.append(jnp.concatenate(split(total), axis=0))
        return u

    def prolong(u, j):
        home = 1 + j // KR
        if j % KR == 0:
            side = u[home - 1]
        elif j % KR == KR - 1:
            side = u[home + 1]
        else:
            up, down = plus[j].astype(BF16), (1.0 - plus[j]).astype(BF16)
            side = u[home - 1] * down + u[home + 1] * up
        value = mm(u[home], coef_ref[j, 0], NN) + mm(side, coef_ref[j, 1], NN)
        return value[:VS] + value[VS:]

    def to_native(src, dst, sem):
        for t in OFFSETS:
            dy, dx = t
            q = lax.rem(odd * COLS + c + 4 * dy + dx, ROWS)
            tr = first_row + lax.div(q, COLS)
            tc = lax.rem(q, COLS)
            if t == (0, 0):
                either(is_diag, src.at[q], dst.at[r], sem, tr, tc)
            else:
                remote(src.at[q], dst.at[r], sem, tr, tc)
        finish_but_one(is_diag, sem, src, ROWS)

    lanes = lax.broadcasted_iota(jnp.int32, (VS, HALF), 1)
    vecs = lax.broadcasted_iota(jnp.int32, (VS, HALF), 0)

    def place(shift):
        return lanes == vecs + VS * shift

    own_place = place(lax.rem(r, 8))

    def as_row(v):
        return jnp.sum(jnp.where(own_place, v, 0.0), axis=0, keepdims=True)

    def as_column(row, mask):
        return jnp.sum(jnp.where(mask, row, 0.0), axis=1, keepdims=True)

    def s_block(j):
        return jnp.concatenate([scol[2 * j], scol[2 * j + 1]], axis=1) * PRESCALE

    def d_block(j):
        return jnp.concatenate([ecol[2 * j], ecol[2 * j + 1]], axis=1) - SHIFT

    def keep(buf, j, v):
        for h in range(2):
            buf[2 * j + h] = v[:, h * HALF:(h + 1) * HALF].astype(BF16)

    def row_sum(v):
        return jnp.sum(v, axis=1, keepdims=True)

    def left_part():
        for i in range(KR):
            for n in range(2):
                cit[i, n] = ci[i, n].T
        for i in range(KR):
            flag = map_ref[1, r * KR + i] == r_next
            row = jnp.where(flag, 8, 0)
            for b in range(4):
                value = mm(cit[i, 0], kbuf[4 + b], NN) + mm(cit[i, 1], kbuf[row + b], NN)
                lbuf[b, pl.ds(i * BANDS, BANDS), :] = value.astype(BF16)

    def tile_piece(j):
        home = 1 + j // KR
        flag = map_ref[1, c * FINE + j] == lax.rem(c * 2 + j // KR + 1, ROWS)
        other = jnp.where(flag, home + 1, home - 1)
        for m in range(KR):
            rows = pl.ds(m * BANDS, BANDS)
            value = mm(lbuf[home, rows], coef_ref[j, 0], NN) + mm(lbuf[other, rows], coef_ref[j, 1], NN)
            tile_ref[rows, pl.ds(j * BANDS, BANDS)] = value.astype(BF16)

    wait_bytes(scol, rsem.at[S])
    restrict([s_block(j) for j in range(FINE)], 0)
    bulk_second()
    coarse_apply(0)
    bulk_third()
    u = reduce_coarse(0)
    wait_bytes(ecol, rsem.at[E])
    parts = []
    ss = sg = gg = jnp.zeros((VS, 1), F32)
    for j in range(FINE):
        s_j = s_block(j)
        y_j = prolong(u, j)
        g_j = y_j + d_block(j) * s_j
        gcol[j] = g_j
        parts.append(g_j)
        keep(y_send, j, y_j)
        ss = ss + row_sum(s_j * s_j)
        sg = sg + row_sum(s_j * g_j)
        gg = gg + row_sum(g_j * g_j)

    restrict(parts, 1)
    for n, v in enumerate((ss, sg, gg)):
        zs_send[n] = as_row(v)
    local(zs_send, zs_recv.at[c], ZS)
    for t in range(1, COLS):
        remote(zs_send, zs_recv.at[c], ZS, r, lax.rem(c + t, COLS))
    finish_plain(ZS, zs_recv.at[pl.ds(0, COLS - 1)])
    column_blocks(1)
    far_piece(1)
    wait_bytes(zs_recv, rsem.at[ZS])
    mean = zs_recv[0]
    for t in range(1, COLS):
        mean = mean + zs_recv[t]
    mean = mean / ORDER
    ss, sg, gg = (as_column(mean[n], own_place) for n in range(3))
    var = ss + EPS * PRESCALE * PRESCALE
    scale = jnp.sqrt(var)
    alpha_one = (sg + SHIFT * ss) / var
    mix = SHIFT - alpha_one
    remain_sq = (gg + 2.0 * mix * sg + mix * mix * ss) / var
    beta = jnp.sqrt(jnp.maximum(remain_sq, 0.0) + EPS)
    inv = 1.0 / (scale * beta)
    over = beta / scale
    for n, v in enumerate((alpha_one, beta, inv, over)):
        ab_send[n] = as_row(v)
    coarse_apply(1)
    for t in OFFSETS:
        if t == (0, 0):
            local(ab_send, ab_recv.at[r], AB)
        else:
            remote(ab_send, ab_recv.at[r], AB, plane_row(t), c)
    finish_plain(AB, ab_recv.at[pl.ds(0, ROWS - 1)])
    to_native(y_send, y_nat, YN)
    bulk_siblings()
    u = reduce_coarse(1)
    dot = jnp.zeros((VS, 1), F32)
    for j in range(FINE):
        s_j = s_block(j)
        g_j = gcol[j]
        z_j = prolong(u, j)
        h_j = z_j + d_block(j) * g_j
        sec = (g_j + mix * s_j) * inv
        shifted = (h_j + mix * g_j) * inv + SHIFT * sec - over * s_j
        dot = dot + row_sum(sec * shifted)
        keep(z_send, j, z_j)
    dot_send[...] = as_row(dot)
    for tz in AROUND:
        for t in OFFSETS:
            if t == (0, 0) and tz == 0:
                local(dot_send, dot_recv.at[c * ROWS + r], DOT)
            else:
                remote(dot_send, dot_recv.at[c * ROWS + r], DOT, plane_row(t), lax.rem(c + tz, COLS))
    finish_plain(DOT, dot_recv.at[pl.ds(0, ROWS * COLS - 1)])
    to_native(z_send, z_nat, ZN)
    bulk_wait()
    left_part()
    for j in range(FINE):
        tile_piece(j)

    wait_bytes(y_nat, rsem.at[YN])
    wait_bytes(ab_recv, rsem.at[AB])
    diag = e_ref[...] - SHIFT
    for i in range(ROWS):
        rows = pl.ds(i * VS, VS)
        mask = place(i % 8)
        first = s_ref[rows, :] * PRESCALE
        image = y_nat[i].astype(F32) + diag * first
        mix_i = SHIFT - as_column(ab_recv[i, 0], mask)
        inv_i = as_column(ab_recv[i, 2], mask)
        over_i = as_column(ab_recv[i, 3], mask)
        sec = (image + mix_i * first) * inv_i
        second_ref[rows, :] = sec
        resid_ref[rows, :] = (diag * image + mix_i * image) * inv_i + SHIFT * sec - over_i * first
    wait_bytes(dot_recv, rsem.at[DOT])
    total = dot_recv[pl.ds(0, ROWS)]
    for t in range(1, COLS):
        total = total + dot_recv[pl.ds(t * ROWS, ROWS)]
    alpha_two = total / ORDER
    lines = []
    for get in (lambda i: ab_recv[i, 0], lambda i: ab_recv[i, 1], lambda i: alpha_two[i]):
        halves = []
        for h in range(2):
            value = get(8 * h)
            for i in range(1, 8):
                value = value + get(8 * h + i)
            halves.append(value)
        lines.append(jnp.concatenate(halves, axis=1))
    coeffs_ref[...] = jnp.concatenate(lines, axis=0)
    wait_bytes(z_nat, rsem.at[ZN])
    for i in range(ROWS):
        rows = pl.ds(i * VS, VS)
        mask = place(i % 8)
        column = as_column(alpha_two[i], mask)
        inv_i = as_column(ab_recv[i, 2], mask)
        resid_ref[rows, :] = resid_ref[rows, :] + z_nat[i].astype(F32) * inv_i - column * second_ref[rows, :]

    for run in finish:
        run()


def write_out(*refs):
    sems = refs[8]
    copies = [pltpu.make_async_copy(refs[n], refs[4 + n], sems.at[n]) for n in range(3)]
    for n in range(8):
        rows = pl.ds(n * 128, 128)
        copies.append(pltpu.make_async_copy(refs[3].at[rows], refs[7].at[rows], sems.at[3 + n]))
    for copy in copies:
        copy.start()
    for copy in copies:
        copy.wait()


def per_device(coarse_kernel, interp_coef, interp_map, energy, start_vectors):
    vmem = pl.BlockSpec(memory_space=pltpu.VMEM)
    hbm = pl.BlockSpec(memory_space=pltpu.HBM)
    nsem = 19 + 8
    shapes = (
        jax.ShapeDtypeStruct((NVEC, HALF), F32),
        jax.ShapeDtypeStruct((NVEC, HALF), F32),
        jax.ShapeDtypeStruct((3, NVEC), F32),
        jax.ShapeDtypeStruct((KR * BANDS, FINE * BANDS), BF16),
    )
    operands = (interp_map.T, coarse_kernel, interp_coef, energy.reshape(1, HALF), start_vectors)
    results = pl.pallas_call(
        kernel,
        out_shape=shapes,
        in_specs=[hbm] * 5,
        out_specs=(vmem, vmem, vmem, vmem),
        scratch_shapes=[
            pltpu.SMEM((2, COLS * FINE), jnp.int32),
            pltpu.VMEM((1, 2, BANDS, BANDS), BF16),
            pltpu.VMEM((FINE, 2, BANDS, BANDS), BF16),
            pltpu.VMEM((1, HALF), F32),
            pltpu.VMEM((NVEC, HALF), F32),
            pltpu.VMEM((16, VS, HALF), F32),
            pltpu.VMEM((16, 1, HALF), F32),
            pltpu.VMEM((FINE, VS, BANDS), F32),
            pltpu.VMEM((12, BANDS, BANDS), BF16),
            pltpu.VMEM((4, 2, BANDS, BANDS), BF16),
            pltpu.VMEM((KR, 2, BANDS, BANDS), BF16),
            pltpu.VMEM((KR, 2, BANDS, BANDS), BF16),
            pltpu.VMEM((4, KR * BANDS, BANDS), BF16),
            pltpu.VMEM((2, VS, 2 * BANDS), BF16),
            pltpu.VMEM((2, 2, VS, BANDS), BF16),
            pltpu.VMEM((2, ROWS, VS, 2 * BANDS), BF16),
            pltpu.VMEM((2, ROWS, VS, BANDS), BF16),
            pltpu.VMEM((2, ROWS, VS, BANDS), BF16),
            pltpu.VMEM((2, ROWS, VS, BANDS), BF16),
            pltpu.VMEM((2, 4 * COLS, VS, BANDS), BF16),
            pltpu.VMEM((3, 1, HALF), F32),
            pltpu.VMEM((COLS, 3, 1, HALF), F32),
            pltpu.VMEM((4, 1, HALF), F32),
            pltpu.VMEM((ROWS, 4, 1, HALF), F32),
            pltpu.VMEM((16, VS, HALF), BF16),
            pltpu.VMEM((16, VS, HALF), BF16),
            pltpu.VMEM((16, VS, HALF), BF16),
            pltpu.VMEM((16, VS, HALF), BF16),
            pltpu.VMEM((1, HALF), F32),
            pltpu.VMEM((COLS * ROWS, 1, HALF), F32),
            pltpu.SemaphoreType.DMA((nsem,)),
            pltpu.SemaphoreType.DMA((nsem,)),
            pltpu.SemaphoreType.DMA((5,)),
        ],
        compiler_params=pltpu.CompilerParams(
            has_side_effects=True, collective_id=0, vmem_limit_bytes=40 * 1024 * 1024
        ),
    )(*(pltpu.with_memory_space_constraint(v, pltpu.HBM) for v in operands))
    return pl.pallas_call(
        write_out,
        out_shape=shapes,
        in_specs=[vmem] * 4,
        out_specs=(hbm,) * 4,
        scratch_shapes=[pltpu.SemaphoreType.DMA((11,))],
        compiler_params=pltpu.CompilerParams(vmem_limit_bytes=1024 * 1024),
    )(*results)


def solution(mesh):
    return jax.shard_map(
        per_device,
        mesh=mesh,
        in_specs=(
            P("row", "col", None, None),
            P("col", None, None, None),
            P(),
            P(("row", "col")),
            P(None, ("row", "col")),
        ),
        out_specs=(P(None, ("row", "col")), P(None, ("row", "col")), P(), P("row", "col")),
        check_vma=False,
    )
```

```python
import jax
import jax.numpy as jnp
from jax import lax
from jax.experimental import pallas as pl
from jax.experimental.pallas import tpu as pltpu
from jax.sharding import PartitionSpec as P

ROWS = 16
COLS = 8
BANDS = 256
NVEC = 256
FINE = 8
KR = 4
VS = NVEC // ROWS
HALF = 128
ORDER = 16384
EPS = 1e-06
PRESCALE = 0.125
SHIFT = 2.0

F32 = jnp.float32
BF16 = jnp.bfloat16
MESH = pl.DeviceIdType.MESH

NT = (((1,), (1,)), ((), ()))
NN = (((1,), (0,)), ((), ()))

OFFSETS = sorted(
    ((dy, dx) for dy in range(4) for dx in range(4)),
    key=lambda t: -(min(t[0], 4 - t[0]) + min(t[1], 4 - t[1])),
)
AROUND = (4, 2, 6, 3, 5, 1, 7, 0)


def groups():
    steps = {t: min(t[0], 4 - t[0]) + min(t[1], 4 - t[1]) for t in OFFSETS}
    return [[t for t in OFFSETS if low <= steps[t] <= high] for low, high in ((0, 1), (2, 2), (3, 4))]


GROUPS = groups()


def mm(a, b, dims):
    return lax.dot_general(a, b, dims, preferred_element_type=F32)


def wait_bytes(ref, sem):
    pltpu.make_async_copy(ref, ref, sem).wait()


def kernel(
    map_hbm, kc_hbm, coef_hbm, e_hbm, s_hbm,
    second_ref, resid_ref, coeffs_ref, tile_ref,
    map_ref, kc_ref, coef_ref, e_ref, s_ref,
    scol, ecol, gcol, kbuf, cj, ci, cit, lbuf,
    wsend, wside, wnear, wfull, usend, ured,
    zs_send, zs_recv, ab_send, ab_recv, y_send, y_nat, z_send, z_nat, dot_send, dot_recv,
    ssem, rsem, lsem,
):
    r = lax.axis_index("row")
    c = lax.axis_index("col")
    z = lax.div(c, 2)
    k = lax.rem(c, 2)
    x = lax.rem(r, 4)
    y = lax.div(r, 4)
    odd = lax.rem(r, 2)
    c_prev = lax.rem(c + COLS - 1, COLS)
    c_next = lax.rem(c + 1, COLS)
    diag_col = lax.div(r, 2)
    near_col = lax.rem(diag_col + COLS - 1 + 2 * odd, COLS)
    is_diag = c == diag_col
    is_near = c == near_col
    first_row = 2 * c
    away = lax.rem(z - y + 4, 4)
    r_next = lax.rem(r + 1, ROWS)
    r_prev = lax.rem(r + ROWS - 1, ROWS)
    sibling = 2 * z + (1 - k)
    finish = []

    loads = []
    for n, (src, dst) in enumerate(((s_hbm, s_ref), (e_hbm, e_ref), (kc_hbm, kc_ref), (coef_hbm, coef_ref), (map_hbm, map_ref))):
        loads.append(pltpu.make_async_copy(src, dst, lsem.at[n]))
        loads[-1].start()

    barrier = pltpu.get_barrier_semaphore()

    def greet(tr, tc):
        pl.semaphore_signal(barrier, inc=1, device_id=(tr, tc), device_id_type=MESH)

    def plane_row(t):
        dy, dx = t
        return 4 * lax.rem(y + dy, 4) + lax.rem(x + dx, 4)

    for q in range(ROWS):
        tr, tc = first_row + q // COLS, q % COLS

        @pl.when(jnp.logical_not(jnp.logical_and(tr == r, tc == c)))
        def _(tr=tr, tc=tc):
            greet(tr, tc)

    for t in range(1, COLS):
        greet(r, lax.rem(c + t, COLS))
    greet(r_next, c)
    greet(r_prev, c)
    pl.semaphore_wait(barrier, 16 + 7 + 2 - is_diag.astype(jnp.int32))

    def remote(src, dst, sem, tr, tc, out=None):
        pltpu.make_async_remote_copy(
            src_ref=src, dst_ref=dst, recv_sem=rsem.at[sem],
            send_sem=ssem.at[sem if out is None else out],
            device_id=(tr, tc), device_id_type=MESH,
        ).start()

    def local(src, dst, sem):
        pltpu.make_async_copy(src, dst, rsem.at[sem]).start()

    def either(here, src, dst, sem, tr, tc, out=None):
        @pl.when(here)
        def _():
            local(src, dst, sem)

        @pl.when(jnp.logical_not(here))
        def _():
            remote(src, dst, sem, tr, tc, out)

    def finish_plain(sem, buf):
        finish.append(lambda: wait_bytes(buf, ssem.at[sem]))

    def finish_but_one(here, sem, buf, count):
        def run():
            @pl.when(here)
            def _():
                wait_bytes(buf.at[pl.ds(0, count - 1)], ssem.at[sem])

            @pl.when(jnp.logical_not(here))
            def _():
                wait_bytes(buf.at[pl.ds(0, count)], ssem.at[sem])

        finish.append(run)

    E, K2, CB, AB, YN, ZN, DOT, ZS = range(8)
    K1, C1, C3, S, HW, APP = 8, 10, 14, 18, 22, 24

    loads[0].wait()
    loads[1].wait()
    for t in OFFSETS:
        tr = plane_row(t)
        src = s_ref.at[pl.ds(pl.multiple_of(tr * VS, VS), VS), :]
        dst = scol.at[odd * COLS + c]
        if t == (0, 0):
            either(is_diag, src, dst, S + away, tr, diag_col, S)
        else:
            remote(src, dst, S + away, tr, diag_col, S)
    finish_but_one(is_diag, S, scol, ROWS)
    for t in OFFSETS:
        tr = plane_row(t)
        dst = ecol.at[odd * COLS + c]
        if t == (0, 0):
            either(is_diag, e_ref, dst, E, tr, diag_col)
        else:
            remote(e_ref, dst, E, tr, diag_col)
    finish_but_one(is_diag, E, ecol, ROWS)
    loads[2].wait()
    loads[3].wait()
    loads[4].wait()

    delta = lax.rem(y - z + 4, 4)
    mine = lax.rem(x, 2) * KR + delta
    home_core = lax.div(x, 2)
    at_source = delta == 0
    serves = k == home_core
    is_home = jnp.logical_and(at_source, serves)
    pair = pl.ds(2 * k, 2)
    piece = [lax.rem(delta + t, 4) for t in range(4)]
    holds = [lax.div(p, 2) == k for p in piece]

    def ring_col(t, core):
        return 2 * lax.rem(z + t, 4) + core

    def row_blocks(b):
        remote(kc_ref.at[0, b], kbuf.at[1 + b], K1 + b, r_next, c)
        remote(kc_ref.at[0, b], kbuf.at[9 + b], K1 + b, r_prev, c)

    def column_blocks(b):
        wait_bytes(kbuf.at[pl.ds(0, 2)], rsem.at[K1 + b])
        for slot in range(3):
            if b == 0:
                remote(kbuf.at[4 * slot + 1], kbuf.at[4 * slot + 3], K2, r, c_prev)
            else:
                remote(kbuf.at[4 * slot + 2], kbuf.at[4 * slot], K2, r, c_next)

    def bulk_first():
        row_blocks(0)

        @pl.when(serves)
        def _():
            for t in (1, 3):
                remote(coef_ref.at[mine], cj.at[t], C1 + t, r, ring_col(t, lax.div(delta, 2)), C1)

    def bulk_second():
        for t in (1, 3):
            @pl.when(holds[t])
            def _(t=t):
                wait_bytes(cj.at[t], rsem.at[C1 + t])
                n = t // 2
                remote(cj.at[t, n], cj.at[2, n], C1 + 2, r, ring_col(t, k), C1 + t)

        column_blocks(0)

    def bulk_third():
        row_blocks(1)

        @pl.when(holds[2])
        def _():
            wait_bytes(cj.at[2], rsem.at[C1 + 2])

        for t in (1, 2, 3):
            @pl.when(jnp.logical_and(holds[t], lax.rem(piece[t], 2) == 1))
            def _(t=t):
                remote(cj.at[t], ci.at[piece[t]], C3, 4 * lax.rem(z + 4 - t, 4) + x, c, C3 + t)

            @pl.when(jnp.logical_and(holds[t], piece[t] == 0))
            def _(t=t):
                local(cj.at[t], ci.at[0], C3)

        far_piece(0)

    def far_piece(n):
        for t in (1, 2, 3):
            @pl.when(jnp.logical_and(holds[t], piece[t] == 2))
            def _(t=t):
                remote(cj.at[t, n], ci.at[2, n], C3, 4 * lax.rem(z + 4 - t, 4) + x, c, C3 + t)

    def bulk_siblings():
        @pl.when(jnp.logical_not(at_source))
        def _():
            wait_bytes(ci.at[pl.ds(0, 2)], rsem.at[C3])
            remote(ci.at[pair], ci.at[pair], CB, r, sibling)

        @pl.when(is_home)
        def _():
            src = coef_ref.at[pl.ds(odd * KR, KR)]
            local(src, ci, C1)
            remote(src, ci, CB, r, sibling)

    def bulk_wait():
        @pl.when(is_home)
        def _():
            wait_bytes(ci, rsem.at[C1])

        @pl.when(jnp.logical_not(at_source))
        def _():
            wait_bytes(ci.at[pl.ds(0, 2)], rsem.at[CB])

        @pl.when(jnp.logical_and(at_source, k != home_core))
        def _():
            wait_bytes(ci, rsem.at[CB])

        wait_bytes(kbuf.at[pl.ds(0, 6)], rsem.at[K2])

    def bulk_finish():
        wait_bytes(kbuf.at[pl.ds(0, 2)], ssem.at[K1])
        wait_bytes(kbuf.at[pl.ds(0, 2)], ssem.at[K1 + 1])
        wait_bytes(kbuf.at[pl.ds(0, 6)], ssem.at[K2])

        @pl.when(serves)
        def _():
            wait_bytes(ci.at[pl.ds(0, 2)], ssem.at[C1])

        for t in (1, 3):
            @pl.when(holds[t])
            def _(t=t):
                wait_bytes(kbuf.at[0], ssem.at[C1 + t])

        for t in (1, 2, 3):
            @pl.when(jnp.logical_and(holds[t], piece[t] != 0))
            def _(t=t):
                wait_bytes(ci.at[0], ssem.at[C3 + t])

        @pl.when(jnp.logical_not(at_source))
        def _():
            wait_bytes(ci.at[pl.ds(0, 2)], ssem.at[CB])

        @pl.when(is_home)
        def _():
            wait_bytes(ci, ssem.at[CB])

    finish.append(bulk_finish)
    bulk_first()
    for b in range(2):
        kbuf[5 + b] = kc_ref[0, b]

    plus = []
    for j in range(FINE):
        home = c * 2 + j // KR
        flag = map_ref[1, c * FINE + j] == lax.rem(home + 1, ROWS)
        plus.append(flag.astype(F32))

    def split(v):
        high = v.astype(BF16)
        return high, (v - high.astype(F32)).astype(BF16)

    def restrict_first():
        acc = [None] * 4

        def add(h, v):
            acc[h] = v if acc[h] is None else acc[h] + v

        for step in (0, 1, 3, 2):
            wait_bytes(scol.at[pl.ds(0, 4)], rsem.at[S + step])
            place_in = lax.rem(z + step, 4)
            for h in range(2):
                j = KR * h + place_in
                value = jnp.concatenate([scol[2 * j], scol[2 * j + 1]], axis=1) * PRESCALE
                both = jnp.concatenate(split(value), axis=0)
                flag = map_ref[1, c * FINE + j] == lax.rem(c * 2 + h + 1, ROWS)
                up = both * flag.astype(F32).astype(BF16)
                add(1 + h, mm(both, coef_ref[j, 0], NT))
                side = mm(jnp.concatenate([both - up, up], axis=0), coef_ref[j, 1], NT)
                add(h, side[:2 * VS])
                add(2 + h, side[2 * VS:])
        spread(acc, 0)

    def restrict(parts, app):
        acc = [None] * 4

        def add(h, v):
            acc[h] = v if acc[h] is None else acc[h] + v

        for j in range(FINE):
            home = 1 + j // KR
            both = jnp.concatenate(split(parts[j]), axis=0)
            add(home, mm(both, coef_ref[j, 0], NT))
            if j % KR == 0:
                add(home - 1, mm(both, coef_ref[j, 1], NT))
            elif j % KR == KR - 1:
                add(home + 1, mm(both, coef_ref[j, 1], NT))
            else:
                up = both * plus[j].astype(BF16)
                side = mm(jnp.concatenate([both - up, up], axis=0), coef_ref[j, 1], NT)
                add(home - 1, side[:2 * VS])
                add(home + 1, side[2 * VS:])
        spread(acc, app)

    def spread(acc, app):
        acc = [v[:VS] + v[VS:] for v in acc]
        sem = HW + app
        wside[app, 0] = acc[0].astype(BF16)
        wside[app, 1] = acc[3].astype(BF16)
        remote(wside.at[app, 0], wnear.at[app, 1], sem, r, c_prev)
        remote(wside.at[app, 1], wnear.at[app, 0], sem, r, c_next)
        finish_plain(sem, wside.at[app])
        wait_bytes(wnear.at[app], rsem.at[sem])
        total = [acc[1 + h] + wnear[app, h].astype(F32) for h in range(2)]
        wsend[app] = jnp.concatenate(total, axis=1).astype(BF16)
        for g in (2, 1, 0):
            sem = APP + 4 * app + g
            for t in GROUPS[g]:
                if t == (0, 0):
                    local(wsend.at[app], wfull.at[app, r], sem)
                else:
                    remote(wsend.at[app], wfull.at[app, r], sem, plane_row(t), c)
            finish_plain(sem, wfull.at[app, pl.ds(0, len(GROUPS[g]) - (g == 0))])

    def coarse_apply(app):
        sem = APP + 4 * app + 3
        for g, group in enumerate(GROUPS):
            wait_bytes(wfull.at[app, pl.ds(0, len(group))], rsem.at[APP + 4 * app + g])
            slots = [plane_row(t) for t in group]
            own = jnp.concatenate([wfull[app, tr] for tr in slots], axis=0)
            part = mm(own[:, :BANDS], kc_ref[0, 0], NT) + mm(own[:, BANDS:], kc_ref[0, 1], NT)
            part = part.astype(BF16)
            for n, tr in enumerate(slots):
                usend[app, tr] = part[n * VS:(n + 1) * VS]
            for t, tr in zip(group, slots):
                src = usend.at[app, tr]
                own = ured.at[app, (1 + odd) * COLS + c]
                near = ured.at[app, 3 * (1 - odd) * COLS + c]
                if t == (0, 0):
                    either(is_diag, src, own, sem, tr, diag_col)
                    either(is_near, src, near, sem, tr, near_col)
                else:
                    remote(src, own, sem, tr, diag_col)
                    remote(src, near, sem, tr, near_col)
        finish_but_one(jnp.logical_or(is_diag, is_near), sem, ured.at[app], 4 * COLS)

    def reduce_coarse(app):
        wait_bytes(ured.at[app], rsem.at[APP + 4 * app + 3])
        u = []
        for h in range(4):
            total = ured[app, h * COLS].astype(F32)
            for t in range(1, COLS):
                total = total + ured[app, h * COLS + t].astype(F32)
            u.append(jnp.concatenate(split(total), axis=0))
        return u

    def prolong(u, j):
        home = 1 + j // KR
        if j % KR == 0:
            side = u[home - 1]
        elif j % KR == KR - 1:
            side = u[home + 1]
        else:
            up, down = plus[j].astype(BF16), (1.0 - plus[j]).astype(BF16)
            side = u[home - 1] * down + u[home + 1] * up
        value = mm(u[home], coef_ref[j, 0], NN) + mm(side, coef_ref[j, 1], NN)
        return value[:VS] + value[VS:]

    def to_native(src, dst, sem):
        for t in OFFSETS:
            dy, dx = t
            q = lax.rem(odd * COLS + c + 4 * dy + dx, ROWS)
            tr = first_row + lax.div(q, COLS)
            tc = lax.rem(q, COLS)
            if t == (0, 0):
                either(is_diag, src.at[q], dst.at[r], sem, tr, tc)
            else:
                remote(src.at[q], dst.at[r], sem, tr, tc)
        finish_but_one(is_diag, sem, src, ROWS)

    lanes = lax.broadcasted_iota(jnp.int32, (VS, HALF), 1)
    vecs = lax.broadcasted_iota(jnp.int32, (VS, HALF), 0)

    def place(shift):
        return lanes == vecs + VS * shift

    own_place = place(lax.rem(r, 8))

    def as_row(v):
        return jnp.sum(jnp.where(own_place, v, 0.0), axis=0, keepdims=True)

    def as_column(row, mask):
        return jnp.sum(jnp.where(mask, row, 0.0), axis=1, keepdims=True)

    def s_block(j):
        return jnp.concatenate([scol[2 * j], scol[2 * j + 1]], axis=1) * PRESCALE

    def d_block(j):
        return jnp.concatenate([ecol[2 * j], ecol[2 * j + 1]], axis=1) - SHIFT

    def keep(buf, j, v):
        for h in range(2):
            buf[2 * j + h] = v[:, h * HALF:(h + 1) * HALF].astype(BF16)

    def row_sum(v):
        return jnp.sum(v, axis=1, keepdims=True)

    def left_part():
        for i in range(KR):
            for n in range(2):
                cit[i, n] = ci[i, n].T
        for i in range(KR):
            flag = map_ref[1, r * KR + i] == r_next
            row = jnp.where(flag, 8, 0)
            for b in range(4):
                value = mm(cit[i, 0], kbuf[4 + b], NN) + mm(cit[i, 1], kbuf[row + b], NN)
                lbuf[b, pl.ds(i * BANDS, BANDS), :] = value.astype(BF16)

    def tile_piece(j):
        home = 1 + j // KR
        flag = map_ref[1, c * FINE + j] == lax.rem(c * 2 + j // KR + 1, ROWS)
        other = jnp.where(flag, home + 1, home - 1)
        for m in range(KR):
            rows = pl.ds(m * BANDS, BANDS)
            value = mm(lbuf[home, rows], coef_ref[j, 0], NN) + mm(lbuf[other, rows], coef_ref[j, 1], NN)
            tile_ref[rows, pl.ds(j * BANDS, BANDS)] = value.astype(BF16)

    restrict_first()
    bulk_second()
    coarse_apply(0)
    bulk_third()
    u = reduce_coarse(0)
    wait_bytes(ecol, rsem.at[E])
    parts = []
    ss = sg = gg = jnp.zeros((VS, 1), F32)
    for j in range(FINE):
        s_j = s_block(j)
        y_j = prolong(u, j)
        g_j = y_j + d_block(j) * s_j
        gcol[j] = g_j
        parts.append(g_j)
        keep(y_send, j, y_j)
        ss = ss + row_sum(s_j * s_j)
        sg = sg + row_sum(s_j * g_j)
        gg = gg + row_sum(g_j * g_j)

    restrict(parts, 1)
    for n, v in enumerate((ss, sg, gg)):
        zs_send[n] = as_row(v)
    local(zs_send, zs_recv.at[c], ZS)
    for t in range(1, COLS):
        remote(zs_send, zs_recv.at[c], ZS, r, lax.rem(c + t, COLS))
    finish_plain(ZS, zs_recv.at[pl.ds(0, COLS - 1)])
    column_blocks(1)
    far_piece(1)
    wait_bytes(zs_recv, rsem.at[ZS])
    mean = zs_recv[0]
    for t in range(1, COLS):
        mean = mean + zs_recv[t]
    mean = mean / ORDER
    ss, sg, gg = (as_column(mean[n], own_place) for n in range(3))
    var = ss + EPS * PRESCALE * PRESCALE
    scale = jnp.sqrt(var)
    alpha_one = (sg + SHIFT * ss) / var
    mix = SHIFT - alpha_one
    remain_sq = (gg + 2.0 * mix * sg + mix * mix * ss) / var
    beta = jnp.sqrt(jnp.maximum(remain_sq, 0.0) + EPS)
    inv = 1.0 / (scale * beta)
    over = beta / scale
    for n, v in enumerate((alpha_one, beta, inv, over)):
        ab_send[n] = as_row(v)
    coarse_apply(1)
    for t in OFFSETS:
        if t == (0, 0):
            local(ab_send, ab_recv.at[r], AB)
        else:
            remote(ab_send, ab_recv.at[r], AB, plane_row(t), c)
    finish_plain(AB, ab_recv.at[pl.ds(0, ROWS - 1)])
    to_native(y_send, y_nat, YN)
    bulk_siblings()
    u = reduce_coarse(1)
    dot = jnp.zeros((VS, 1), F32)
    for j in range(FINE):
        s_j = s_block(j)
        g_j = gcol[j]
        z_j = prolong(u, j)
        h_j = z_j + d_block(j) * g_j
        sec = (g_j + mix * s_j) * inv
        shifted = (h_j + mix * g_j) * inv + SHIFT * sec - over * s_j
        dot = dot + row_sum(sec * shifted)
        keep(z_send, j, z_j)
    dot_send[...] = as_row(dot)
    for tz in AROUND:
        for t in OFFSETS:
            if t == (0, 0) and tz == 0:
                local(dot_send, dot_recv.at[c * ROWS + r], DOT)
            else:
                remote(dot_send, dot_recv.at[c * ROWS + r], DOT, plane_row(t), lax.rem(c + tz, COLS))
    finish_plain(DOT, dot_recv.at[pl.ds(0, ROWS * COLS - 1)])
    to_native(z_send, z_nat, ZN)
    bulk_wait()
    left_part()
    for j in range(FINE):
        tile_piece(j)

    wait_bytes(y_nat, rsem.at[YN])
    wait_bytes(ab_recv, rsem.at[AB])
    diag = e_ref[...] - SHIFT
    for i in range(ROWS):
        rows = pl.ds(i * VS, VS)
        mask = place(i % 8)
        first = s_ref[rows, :] * PRESCALE
        image = y_nat[i].astype(F32) + diag * first
        mix_i = SHIFT - as_column(ab_recv[i, 0], mask)
        inv_i = as_column(ab_recv[i, 2], mask)
        over_i = as_column(ab_recv[i, 3], mask)
        sec = (image + mix_i * first) * inv_i
        second_ref[rows, :] = sec
        resid_ref[rows, :] = (diag * image + mix_i * image) * inv_i + SHIFT * sec - over_i * first
    wait_bytes(dot_recv, rsem.at[DOT])
    total = dot_recv[pl.ds(0, ROWS)]
    for t in range(1, COLS):
        total = total + dot_recv[pl.ds(t * ROWS, ROWS)]
    alpha_two = total / ORDER
    lines = []
    for get in (lambda i: ab_recv[i, 0], lambda i: ab_recv[i, 1], lambda i: alpha_two[i]):
        halves = []
        for h in range(2):
            value = get(8 * h)
            for i in range(1, 8):
                value = value + get(8 * h + i)
            halves.append(value)
        lines.append(jnp.concatenate(halves, axis=1))
    coeffs_ref[...] = jnp.concatenate(lines, axis=0)
    wait_bytes(z_nat, rsem.at[ZN])
    for i in range(ROWS):
        rows = pl.ds(i * VS, VS)
        mask = place(i % 8)
        column = as_column(alpha_two[i], mask)
        inv_i = as_column(ab_recv[i, 2], mask)
        resid_ref[rows, :] = resid_ref[rows, :] + z_nat[i].astype(F32) * inv_i - column * second_ref[rows, :]

    for run in finish:
        run()


def write_out(*refs):
    sems = refs[8]
    copies = [pltpu.make_async_copy(refs[n], refs[4 + n], sems.at[n]) for n in range(3)]
    for n in range(8):
        rows = pl.ds(n * 128, 128)
        copies.append(pltpu.make_async_copy(refs[3].at[rows], refs[7].at[rows], sems.at[3 + n]))
    for copy in copies:
        copy.start()
    for copy in copies:
        copy.wait()


def per_device(coarse_kernel, interp_coef, interp_map, energy, start_vectors):
    vmem = pl.BlockSpec(memory_space=pltpu.VMEM)
    hbm = pl.BlockSpec(memory_space=pltpu.HBM)
    nsem = 24 + 8
    shapes = (
        jax.ShapeDtypeStruct((NVEC, HALF), F32),
        jax.ShapeDtypeStruct((NVEC, HALF), F32),
        jax.ShapeDtypeStruct((3, NVEC), F32),
        jax.ShapeDtypeStruct((KR * BANDS, FINE * BANDS), BF16),
    )
    operands = (interp_map.T, coarse_kernel, interp_coef, energy.reshape(1, HALF), start_vectors)
    results = pl.pallas_call(
        kernel,
        out_shape=shapes,
        in_specs=[hbm] * 5,
        out_specs=(vmem, vmem, vmem, vmem),
        scratch_shapes=[
            pltpu.SMEM((2, COLS * FINE), jnp.int32),
            pltpu.VMEM((1, 2, BANDS, BANDS), BF16),
            pltpu.VMEM((FINE, 2, BANDS, BANDS), BF16),
            pltpu.VMEM((1, HALF), F32),
            pltpu.VMEM((NVEC, HALF), F32),
            pltpu.VMEM((16, VS, HALF), F32),
            pltpu.VMEM((16, 1, HALF), F32),
            pltpu.VMEM((FINE, VS, BANDS), F32),
            pltpu.VMEM((12, BANDS, BANDS), BF16),
            pltpu.VMEM((4, 2, BANDS, BANDS), BF16),
            pltpu.VMEM((KR, 2, BANDS, BANDS), BF16),
            pltpu.VMEM((KR, 2, BANDS, BANDS), BF16),
            pltpu.VMEM((4, KR * BANDS, BANDS), BF16),
            pltpu.VMEM((2, VS, 2 * BANDS), BF16),
            pltpu.VMEM((2, 2, VS, BANDS), BF16),
            pltpu.VMEM((2, 2, VS, BANDS), BF16),
            pltpu.VMEM((2, ROWS, VS, 2 * BANDS), BF16),
            pltpu.VMEM((2, ROWS, VS, BANDS), BF16),
            pltpu.VMEM((2, 4 * COLS, VS, BANDS), BF16),
            pltpu.VMEM((3, 1, HALF), F32),
            pltpu.VMEM((COLS, 3, 1, HALF), F32),
            pltpu.VMEM((4, 1, HALF), F32),
            pltpu.VMEM((ROWS, 4, 1, HALF), F32),
            pltpu.VMEM((16, VS, HALF), BF16),
            pltpu.VMEM((16, VS, HALF), BF16),
            pltpu.VMEM((16, VS, HALF), BF16),
            pltpu.VMEM((16, VS, HALF), BF16),
            pltpu.VMEM((1, HALF), F32),
            pltpu.VMEM((COLS * ROWS, 1, HALF), F32),
            pltpu.SemaphoreType.DMA((nsem,)),
            pltpu.SemaphoreType.DMA((nsem,)),
            pltpu.SemaphoreType.DMA((5,)),
        ],
        compiler_params=pltpu.CompilerParams(
            has_side_effects=True, collective_id=0, vmem_limit_bytes=40 * 1024 * 1024
        ),
    )(*(pltpu.with_memory_space_constraint(v, pltpu.HBM) for v in operands))
    return pl.pallas_call(
        write_out,
        out_shape=shapes,
        in_specs=[vmem] * 4,
        out_specs=(hbm,) * 4,
        scratch_shapes=[pltpu.SemaphoreType.DMA((11,))],
        compiler_params=pltpu.CompilerParams(vmem_limit_bytes=1024 * 1024),
    )(*results)


def solution(mesh):
    return jax.shard_map(
        per_device,
        mesh=mesh,
        in_specs=(
            P("row", "col", None, None),
            P("col", None, None, None),
            P(),
            P(("row", "col")),
            P(None, ("row", "col")),
        ),
        out_specs=(P(None, ("row", "col")), P(None, ("row", "col")), P(), P("row", "col")),
        check_vma=False,
    )
```

```python
import jax
import jax.numpy as jnp
from jax import lax
from jax.experimental import pallas as pl
from jax.experimental.pallas import tpu as pltpu
from jax.sharding import PartitionSpec as P

ROWS = 16
COLS = 8
BANDS = 256
NVEC = 256
FINE = 8
KR = 4
VS = NVEC // ROWS
HALF = 128
ORDER = 16384
EPS = 1e-06
PRESCALE = 0.125
SHIFT = 2.0

F32 = jnp.float32
BF16 = jnp.bfloat16
MESH = pl.DeviceIdType.MESH

NT = (((1,), (1,)), ((), ()))
NN = (((1,), (0,)), ((), ()))

OFFSETS = sorted(
    ((dy, dx) for dy in range(4) for dx in range(4)),
    key=lambda t: -(min(t[0], 4 - t[0]) + min(t[1], 4 - t[1])),
)
AROUND = (4, 2, 6, 3, 5, 1, 7, 0)


def groups():
    steps = {t: min(t[0], 4 - t[0]) + min(t[1], 4 - t[1]) for t in OFFSETS}
    return [[t for t in OFFSETS if low <= steps[t] <= high] for low, high in ((0, 1), (2, 2), (3, 4))]


GROUPS = groups()


def mm(a, b, dims):
    return lax.dot_general(a, b, dims, preferred_element_type=F32)


def wait_bytes(ref, sem):
    pltpu.make_async_copy(ref, ref, sem).wait()


def kernel(
    map_hbm, kc_hbm, coef_hbm, e_hbm, s_hbm,
    second_ref, resid_ref, coeffs_ref, tile_ref,
    map_ref, kc_ref, coef_ref, e_ref, s_ref,
    scol, ecol, kbuf, cj, ci, cit, lbuf,
    wsend, wside, wnear, wfull, usend, ured,
    zs_send, zs_recv, ab_send, ab_recv, y_send, y_nat, zred, wdot, usum, uside, z_send, z_nat, dot_send, dot_recv,
    ssem, rsem, lsem,
):
    r = lax.axis_index("row")
    c = lax.axis_index("col")
    z = lax.div(c, 2)
    k = lax.rem(c, 2)
    x = lax.rem(r, 4)
    y = lax.div(r, 4)
    odd = lax.rem(r, 2)
    c_prev = lax.rem(c + COLS - 1, COLS)
    c_next = lax.rem(c + 1, COLS)
    diag_col = lax.div(r, 2)
    near_col = lax.rem(diag_col + COLS - 1 + 2 * odd, COLS)
    is_diag = c == diag_col
    is_near = c == near_col
    first_row = 2 * c
    away = lax.rem(z - y + 4, 4)
    r_next = lax.rem(r + 1, ROWS)
    r_prev = lax.rem(r + ROWS - 1, ROWS)
    sibling = 2 * z + (1 - k)
    finish = []

    loads = []
    for n, (src, dst) in enumerate(((s_hbm, s_ref), (e_hbm, e_ref), (kc_hbm, kc_ref), (coef_hbm, coef_ref), (map_hbm, map_ref))):
        loads.append(pltpu.make_async_copy(src, dst, lsem.at[n]))
        loads[-1].start()

    barrier = pltpu.get_barrier_semaphore()

    def greet(tr, tc):
        pl.semaphore_signal(barrier, inc=1, device_id=(tr, tc), device_id_type=MESH)

    def plane_row(t):
        dy, dx = t
        return 4 * lax.rem(y + dy, 4) + lax.rem(x + dx, 4)

    for q in range(ROWS):
        tr, tc = first_row + q // COLS, q % COLS

        @pl.when(jnp.logical_not(jnp.logical_and(tr == r, tc == c)))
        def _(tr=tr, tc=tc):
            greet(tr, tc)

    for t in range(1, COLS):
        greet(r, lax.rem(c + t, COLS))
    greet(r_next, c)
    greet(r_prev, c)
    pl.semaphore_wait(barrier, 16 + 7 + 2 - is_diag.astype(jnp.int32))

    def remote(src, dst, sem, tr, tc, out=None):
        pltpu.make_async_remote_copy(
            src_ref=src, dst_ref=dst, recv_sem=rsem.at[sem],
            send_sem=ssem.at[sem if out is None else out],
            device_id=(tr, tc), device_id_type=MESH,
        ).start()

    def local(src, dst, sem):
        pltpu.make_async_copy(src, dst, rsem.at[sem]).start()

    def either(here, src, dst, sem, tr, tc, out=None):
        @pl.when(here)
        def _():
            local(src, dst, sem)

        @pl.when(jnp.logical_not(here))
        def _():
            remote(src, dst, sem, tr, tc, out)

    def finish_plain(sem, buf):
        finish.append(lambda: wait_bytes(buf, ssem.at[sem]))

    def finish_but_one(here, sem, buf, count):
        def run():
            @pl.when(here)
            def _():
                wait_bytes(buf.at[pl.ds(0, count - 1)], ssem.at[sem])

            @pl.when(jnp.logical_not(here))
            def _():
                wait_bytes(buf.at[pl.ds(0, count)], ssem.at[sem])

        finish.append(run)

    E, K2, CB, AB, YN, WD, UN, ZN, DOT, ZS = range(10)
    K1, C1, C3, S, HW, APP = 10, 12, 16, 20, 24, 26

    loads[0].wait()
    loads[1].wait()
    for t in OFFSETS:
        tr = plane_row(t)
        src = s_ref.at[pl.ds(pl.multiple_of(tr * VS, VS), VS), :]
        dst = scol.at[odd * COLS + c]
        if t == (0, 0):
            either(is_diag, src, dst, S + away, tr, diag_col, S)
        else:
            remote(src, dst, S + away, tr, diag_col, S)
    finish_but_one(is_diag, S, scol, ROWS)
    for t in OFFSETS:
        tr = plane_row(t)
        dst = ecol.at[odd * COLS + c]
        if t == (0, 0):
            either(is_diag, e_ref, dst, E, tr, diag_col)
        else:
            remote(e_ref, dst, E, tr, diag_col)
    finish_but_one(is_diag, E, ecol, ROWS)
    loads[2].wait()
    loads[3].wait()
    loads[4].wait()

    delta = lax.rem(y - z + 4, 4)
    mine = lax.rem(x, 2) * KR + delta
    home_core = lax.div(x, 2)
    at_source = delta == 0
    serves = k == home_core
    is_home = jnp.logical_and(at_source, serves)
    pair = pl.ds(2 * k, 2)
    piece = [lax.rem(delta + t, 4) for t in range(4)]
    holds = [lax.div(p, 2) == k for p in piece]

    def ring_col(t, core):
        return 2 * lax.rem(z + t, 4) + core

    def row_blocks(b):
        remote(kc_ref.at[0, b], kbuf.at[1 + b], K1 + b, r_next, c)
        remote(kc_ref.at[0, b], kbuf.at[9 + b], K1 + b, r_prev, c)

    def column_blocks(b):
        wait_bytes(kbuf.at[pl.ds(0, 2)], rsem.at[K1 + b])
        for slot in range(3):
            if b == 0:
                remote(kbuf.at[4 * slot + 1], kbuf.at[4 * slot + 3], K2, r, c_prev)
            else:
                remote(kbuf.at[4 * slot + 2], kbuf.at[4 * slot], K2, r, c_next)

    def bulk_first():
        row_blocks(0)

        @pl.when(serves)
        def _():
            for t in (1, 3):
                remote(coef_ref.at[mine], cj.at[t], C1 + t, r, ring_col(t, lax.div(delta, 2)), C1)

    def bulk_second():
        for t in (1, 3):
            @pl.when(holds[t])
            def _(t=t):
                wait_bytes(cj.at[t], rsem.at[C1 + t])
                n = t // 2
                remote(cj.at[t, n], cj.at[2, n], C1 + 2, r, ring_col(t, k), C1 + t)

        column_blocks(0)

    def bulk_third():
        row_blocks(1)

        @pl.when(holds[2])
        def _():
            wait_bytes(cj.at[2], rsem.at[C1 + 2])

        for t in (1, 2, 3):
            @pl.when(jnp.logical_and(holds[t], lax.rem(piece[t], 2) == 1))
            def _(t=t):
                remote(cj.at[t], ci.at[piece[t]], C3, 4 * lax.rem(z + 4 - t, 4) + x, c, C3 + t)

            @pl.when(jnp.logical_and(holds[t], piece[t] == 0))
            def _(t=t):
                local(cj.at[t], ci.at[0], C3)

        far_piece(0)

    def far_piece(n):
        for t in (1, 2, 3):
            @pl.when(jnp.logical_and(holds[t], piece[t] == 2))
            def _(t=t):
                remote(cj.at[t, n], ci.at[2, n], C3, 4 * lax.rem(z + 4 - t, 4) + x, c, C3 + t)

    def bulk_siblings():
        @pl.when(jnp.logical_not(at_source))
        def _():
            wait_bytes(ci.at[pl.ds(0, 2)], rsem.at[C3])
            remote(ci.at[pair], ci.at[pair], CB, r, sibling)

        @pl.when(is_home)
        def _():
            src = coef_ref.at[pl.ds(odd * KR, KR)]
            local(src, ci, C1)
            remote(src, ci, CB, r, sibling)

    def bulk_wait():
        @pl.when(is_home)
        def _():
            wait_bytes(ci, rsem.at[C1])

        @pl.when(jnp.logical_not(at_source))
        def _():
            wait_bytes(ci.at[pl.ds(0, 2)], rsem.at[CB])

        @pl.when(jnp.logical_and(at_source, k != home_core))
        def _():
            wait_bytes(ci, rsem.at[CB])

        wait_bytes(kbuf.at[pl.ds(0, 6)], rsem.at[K2])

    def bulk_finish():
        wait_bytes(kbuf.at[pl.ds(0, 2)], ssem.at[K1])
        wait_bytes(kbuf.at[pl.ds(0, 2)], ssem.at[K1 + 1])
        wait_bytes(kbuf.at[pl.ds(0, 6)], ssem.at[K2])

        @pl.when(serves)
        def _():
            wait_bytes(ci.at[pl.ds(0, 2)], ssem.at[C1])

        for t in (1, 3):
            @pl.when(holds[t])
            def _(t=t):
                wait_bytes(kbuf.at[0], ssem.at[C1 + t])

        for t in (1, 2, 3):
            @pl.when(jnp.logical_and(holds[t], piece[t] != 0))
            def _(t=t):
                wait_bytes(ci.at[0], ssem.at[C3 + t])

        @pl.when(jnp.logical_not(at_source))
        def _():
            wait_bytes(ci.at[pl.ds(0, 2)], ssem.at[CB])

        @pl.when(is_home)
        def _():
            wait_bytes(ci, ssem.at[CB])

    finish.append(bulk_finish)
    bulk_first()
    for b in range(2):
        kbuf[5 + b] = kc_ref[0, b]

    plus = []
    for j in range(FINE):
        home = c * 2 + j // KR
        flag = map_ref[1, c * FINE + j] == lax.rem(home + 1, ROWS)
        plus.append(flag.astype(F32))

    def split(v):
        high = v.astype(BF16)
        return high, (v - high.astype(F32)).astype(BF16)

    def restrict_first():
        acc = [None] * 4

        def add(h, v):
            acc[h] = v if acc[h] is None else acc[h] + v

        for step in (0, 1, 3, 2):
            wait_bytes(scol.at[pl.ds(0, 4)], rsem.at[S + step])
            place_in = lax.rem(z + step, 4)
            for h in range(2):
                j = KR * h + place_in
                value = jnp.concatenate([scol[2 * j], scol[2 * j + 1]], axis=1) * PRESCALE
                both = jnp.concatenate(split(value), axis=0)
                flag = map_ref[1, c * FINE + j] == lax.rem(c * 2 + h + 1, ROWS)
                up = both * flag.astype(F32).astype(BF16)
                add(1 + h, mm(both, coef_ref[j, 0], NT))
                side = mm(jnp.concatenate([both - up, up], axis=0), coef_ref[j, 1], NT)
                add(h, side[:2 * VS])
                add(2 + h, side[2 * VS:])
        spread(acc, 0)

    def restrict(parts, app):
        acc = [None] * 4

        def add(h, v):
            acc[h] = v if acc[h] is None else acc[h] + v

        for j in range(FINE):
            home = 1 + j // KR
            both = jnp.concatenate(split(parts[j]), axis=0)
            add(home, mm(both, coef_ref[j, 0], NT))
            if j % KR == 0:
                add(home - 1, mm(both, coef_ref[j, 1], NT))
            elif j % KR == KR - 1:
                add(home + 1, mm(both, coef_ref[j, 1], NT))
            else:
                up = both * plus[j].astype(BF16)
                side = mm(jnp.concatenate([both - up, up], axis=0), coef_ref[j, 1], NT)
                add(home - 1, side[:2 * VS])
                add(home + 1, side[2 * VS:])
        spread(acc, app)

    def spread(acc, app):
        acc = [v[:VS] + v[VS:] for v in acc]
        sem = HW + app
        wside[app, 0] = acc[0].astype(BF16)
        wside[app, 1] = acc[3].astype(BF16)
        remote(wside.at[app, 0], wnear.at[app, 1], sem, r, c_prev)
        remote(wside.at[app, 1], wnear.at[app, 0], sem, r, c_next)
        finish_plain(sem, wside.at[app])
        wait_bytes(wnear.at[app], rsem.at[sem])
        total = [acc[1 + h] + wnear[app, h].astype(F32) for h in range(2)]
        wsend[app] = jnp.concatenate(total, axis=1).astype(BF16)
        for g in (2, 1, 0):
            sem = APP + 4 * app + g
            for t in GROUPS[g]:
                if t == (0, 0):
                    local(wsend.at[app], wfull.at[app, r], sem)
                else:
                    remote(wsend.at[app], wfull.at[app, r], sem, plane_row(t), c)
            finish_plain(sem, wfull.at[app, pl.ds(0, len(GROUPS[g]) - (g == 0))])

    def coarse_apply(app):
        sem = APP + 4 * app + 3
        for g, group in enumerate(GROUPS):
            wait_bytes(wfull.at[app, pl.ds(0, len(group))], rsem.at[APP + 4 * app + g])
            slots = [plane_row(t) for t in group]
            own = jnp.concatenate([wfull[app, tr] for tr in slots], axis=0)
            part = mm(own[:, :BANDS], kc_ref[0, 0], NT) + mm(own[:, BANDS:], kc_ref[0, 1], NT)
            part = part.astype(BF16)
            for n, tr in enumerate(slots):
                usend[app, tr] = part[n * VS:(n + 1) * VS]
            for t, tr in zip(group, slots):
                src = usend.at[app, tr]
                if app:
                    half = lax.div(tr, 2)
                    either(half == c, src, zred.at[c, lax.rem(tr, 2)], sem, r, half)
                    continue
                own = ured.at[(1 + odd) * COLS + c]
                near = ured.at[3 * (1 - odd) * COLS + c]
                if t == (0, 0):
                    either(is_diag, src, own, sem, tr, diag_col)
                    either(is_near, src, near, sem, tr, near_col)
                else:
                    remote(src, own, sem, tr, diag_col)
                    remote(src, near, sem, tr, near_col)
        if app:
            finish_plain(sem, usend.at[app, pl.ds(0, ROWS - 2)])
        else:
            finish_but_one(jnp.logical_or(is_diag, is_near), sem, ured, 4 * COLS)

    def reduce_coarse():
        wait_bytes(ured, rsem.at[APP + 3])
        u = []
        for h in range(4):
            total = ured[h * COLS].astype(F32)
            for t in range(1, COLS):
                total = total + ured[h * COLS + t].astype(F32)
            u.append(jnp.concatenate(split(total), axis=0))
        return u

    def prolong(u, j):
        home = 1 + j // KR
        if j % KR == 0:
            side = u[home - 1]
        elif j % KR == KR - 1:
            side = u[home + 1]
        else:
            up, down = plus[j].astype(BF16), (1.0 - plus[j]).astype(BF16)
            side = u[home - 1] * down + u[home + 1] * up
        value = mm(u[home], coef_ref[j, 0], NN) + mm(side, coef_ref[j, 1], NN)
        return value[:VS] + value[VS:]

    def to_native(src, dst, sem):
        for t in OFFSETS:
            dy, dx = t
            q = lax.rem(odd * COLS + c + 4 * dy + dx, ROWS)
            tr = first_row + lax.div(q, COLS)
            tc = lax.rem(q, COLS)
            if t == (0, 0):
                either(is_diag, src.at[q], dst.at[r], sem, tr, tc)
            else:
                remote(src.at[q], dst.at[r], sem, tr, tc)
        finish_but_one(is_diag, sem, src, ROWS)

    lanes = lax.broadcasted_iota(jnp.int32, (VS, HALF), 1)
    vecs = lax.broadcasted_iota(jnp.int32, (VS, HALF), 0)

    def place(shift):
        return lanes == vecs + VS * shift

    own_place = place(lax.rem(r, 8))

    lane_group = lax.div(lax.broadcasted_iota(jnp.int32, (1, HALF), 1), VS)

    def place_row(shift):
        return lane_group == shift

    def as_row(v):
        return jnp.sum(jnp.where(own_place, v, 0.0), axis=0, keepdims=True)

    def as_column(row, mask):
        return jnp.sum(jnp.where(mask, row, 0.0), axis=1, keepdims=True)

    def s_block(j):
        return jnp.concatenate([scol[2 * j], scol[2 * j + 1]], axis=1) * PRESCALE

    def d_block(j):
        return jnp.concatenate([ecol[2 * j], ecol[2 * j + 1]], axis=1) - SHIFT

    def keep(buf, j, v):
        for h in range(2):
            buf[2 * j + h] = v[:, h * HALF:(h + 1) * HALF].astype(BF16)

    def row_sum(v):
        return jnp.sum(v, axis=1, keepdims=True)

    def left_part():
        for i in range(KR):
            for n in range(2):
                cit[i, n] = ci[i, n].T
        for i in range(KR):
            flag = map_ref[1, r * KR + i] == r_next
            row = jnp.where(flag, 8, 0)
            for b in range(4):
                value = mm(cit[i, 0], kbuf[4 + b], NN) + mm(cit[i, 1], kbuf[row + b], NN)
                lbuf[b, pl.ds(i * BANDS, BANDS), :] = value.astype(BF16)

    def tile_piece(j):
        home = 1 + j // KR
        flag = map_ref[1, c * FINE + j] == lax.rem(c * 2 + j // KR + 1, ROWS)
        other = jnp.where(flag, home + 1, home - 1)
        for m in range(KR):
            rows = pl.ds(m * BANDS, BANDS)
            value = mm(lbuf[home, rows], coef_ref[j, 0], NN) + mm(lbuf[other, rows], coef_ref[j, 1], NN)
            tile_ref[rows, pl.ds(j * BANDS, BANDS)] = value.astype(BF16)

    restrict_first()
    bulk_second()
    coarse_apply(0)
    bulk_third()
    u = reduce_coarse()
    wait_bytes(ecol, rsem.at[E])
    parts = []
    ss = sg = gg = gdg = jnp.zeros((VS, 1), F32)
    for j in range(FINE):
        s_j = s_block(j)
        y_j = prolong(u, j)
        g_j = y_j + d_block(j) * s_j
        parts.append(g_j)
        keep(y_send, j, y_j)
        ss = ss + row_sum(s_j * s_j)
        sg = sg + row_sum(s_j * g_j)
        gg = gg + row_sum(g_j * g_j)
        gdg = gdg + row_sum(g_j * g_j * d_block(j))

    restrict(parts, 1)
    for h in range(2):
        src = wsend.at[1, :, pl.ds(h * BANDS, BANDS)]
        either(jnp.logical_and(is_diag, odd == h), src, wdot.at[odd], WD, first_row + h, diag_col)
    finish_but_one(is_diag, WD, wdot, 2)
    for n, v in enumerate((ss, sg, gg, gdg)):
        zs_send[n] = as_row(v)
    local(zs_send, zs_recv.at[c], ZS)
    for t in range(1, COLS):
        remote(zs_send, zs_recv.at[c], ZS, r, lax.rem(c + t, COLS))
    finish_plain(ZS, zs_recv.at[pl.ds(0, COLS - 1)])
    column_blocks(1)
    far_piece(1)
    wait_bytes(zs_recv, rsem.at[ZS])
    mean = zs_recv[0]
    for t in range(1, COLS):
        mean = mean + zs_recv[t]
    mean = mean / ORDER
    ss, sg, gg, gdg = (as_column(mean[n], own_place) for n in range(4))
    var = ss + EPS * PRESCALE * PRESCALE
    scale = jnp.sqrt(var)
    alpha_one = (sg + SHIFT * ss) / var
    mix = SHIFT - alpha_one
    remain_sq = (gg + 2.0 * mix * sg + mix * mix * ss) / var
    beta = jnp.sqrt(jnp.maximum(remain_sq, 0.0) + EPS)
    inv = 1.0 / (scale * beta)
    over = beta / scale
    sec_sec = (gg + 2.0 * mix * sg + mix * mix * ss) * inv * inv
    known = (gdg + 2.0 * mix * gg + mix * mix * sg) * inv * inv + SHIFT * sec_sec
    known = known - over * inv * (sg + mix * ss)
    for n, v in enumerate((alpha_one, beta, inv, over, known)):
        ab_send[n] = as_row(v)
    coarse_apply(1)
    for t in OFFSETS:
        if t == (0, 0):
            local(ab_send, ab_recv.at[r], AB)
        else:
            remote(ab_send, ab_recv.at[r], AB, plane_row(t), c)
    finish_plain(AB, ab_recv.at[pl.ds(0, ROWS - 1)])
    to_native(y_send, y_nat, YN)
    bulk_siblings()

    wait_bytes(zred, rsem.at[APP + 7])
    wait_bytes(wdot, rsem.at[WD])
    line, own_u = None, []
    for h in range(2):
        total = zred[0, h].astype(F32)
        for t in range(1, COLS):
            total = total + zred[t, h].astype(F32)
        own_u.append(total)
        usum[pl.ds(h * VS, VS), :] = total.astype(BF16)
        inner = row_sum(total * wdot[h].astype(F32))
        row = jnp.sum(jnp.where(place(2 * lax.rem(c, 4) + h), inner, 0.0), axis=0, keepdims=True)
        line = row if line is None else line + row
    remote(usum, uside.at[0], UN, r_next, c)
    remote(usum, uside.at[1], UN, r_prev, c)
    finish_plain(UN, uside)
    own_u = jnp.concatenate(split(jnp.concatenate(own_u, axis=0)), axis=0)
    dot_send[...] = line
    for tz in AROUND:
        for t in OFFSETS:
            if t == (0, 0) and tz == 0:
                local(dot_send, dot_recv.at[c * ROWS + r], DOT)
            else:
                remote(dot_send, dot_recv.at[c * ROWS + r], DOT, plane_row(t), lax.rem(c + tz, COLS))
    finish_plain(DOT, dot_recv.at[pl.ds(0, ROWS * COLS - 1)])
    bulk_wait()
    left_part()

    wait_bytes(uside, rsem.at[UN])
    for i in range(KR):
        if i == 0:
            side = uside[0]
        elif i == KR - 1:
            side = uside[1]
        else:
            up = (map_ref[1, r * KR + i] == r_next).astype(F32)
            side = uside[0] * (1.0 - up).astype(BF16) + uside[1] * up.astype(BF16)
        value = mm(own_u, ci[i, 0], NN)
        value = value[:2 * VS] + value[2 * VS:] + mm(side, ci[i, 1], NN)
        for h in range(2):
            z_send[2 * i + h] = value[:, h * HALF:(h + 1) * HALF].astype(BF16)
    for tz in AROUND:
        tc = lax.rem(c + tz, COLS)
        if tz == 0:
            local(z_send.at[tc], z_nat.at[c], ZN)
        else:
            remote(z_send.at[tc], z_nat.at[c], ZN, r, tc)
    finish_plain(ZN, z_send.at[pl.ds(0, COLS - 1)])
    for j in range(FINE):
        tile_piece(j)

    wait_bytes(y_nat, rsem.at[YN])
    wait_bytes(ab_recv, rsem.at[AB])
    diag = e_ref[...] - SHIFT
    for i in range(ROWS):
        rows = pl.ds(i * VS, VS)
        mask = place(i % 8)
        first = s_ref[rows, :] * PRESCALE
        image = y_nat[i].astype(F32) + diag * first
        mix_i = SHIFT - as_column(ab_recv[i, 0], mask)
        inv_i = as_column(ab_recv[i, 2], mask)
        over_i = as_column(ab_recv[i, 3], mask)
        sec = (image + mix_i * first) * inv_i
        second_ref[rows, :] = sec
        resid_ref[rows, :] = (diag * image + mix_i * image) * inv_i + SHIFT * sec - over_i * first
    wait_bytes(z_nat, rsem.at[ZN])
    image_two = z_nat[...].reshape(NVEC, HALF).astype(F32)
    wait_bytes(dot_recv, rsem.at[DOT])
    inner = []
    for h in range(2):
        total = dot_recv[h * 4 * ROWS]
        for t in range(1, 4 * ROWS):
            total = total + dot_recv[h * 4 * ROWS + t]
        inner.append(total / ORDER)

    def second_alpha(i):
        inv_row = ab_recv[i, 2]
        return ab_recv[i, 4] + jnp.where(place_row(i % 8), inner[i // 8], 0.0) * inv_row * inv_row

    alpha_two = [second_alpha(i) for i in range(ROWS)]
    lines = []
    for get in (lambda i: ab_recv[i, 0], lambda i: ab_recv[i, 1], lambda i: alpha_two[i]):
        halves = []
        for h in range(2):
            value = get(8 * h)
            for i in range(1, 8):
                value = value + get(8 * h + i)
            halves.append(value)
        lines.append(jnp.concatenate(halves, axis=1))
    coeffs_ref[...] = jnp.concatenate(lines, axis=0)
    for i in range(ROWS):
        rows = pl.ds(i * VS, VS)
        mask = place(i % 8)
        column = as_column(alpha_two[i], mask)
        inv_i = as_column(ab_recv[i, 2], mask)
        resid_ref[rows, :] = resid_ref[rows, :] + image_two[i * VS:(i + 1) * VS] * inv_i - column * second_ref[rows, :]

    for run in finish:
        run()


def write_out(*refs):
    sems = refs[8]
    copies = [pltpu.make_async_copy(refs[n], refs[4 + n], sems.at[n]) for n in range(3)]
    for n in range(8):
        rows = pl.ds(n * 128, 128)
        copies.append(pltpu.make_async_copy(refs[3].at[rows], refs[7].at[rows], sems.at[3 + n]))
    for copy in copies:
        copy.start()
    for copy in copies:
        copy.wait()


def per_device(coarse_kernel, interp_coef, interp_map, energy, start_vectors):
    vmem = pl.BlockSpec(memory_space=pltpu.VMEM)
    hbm = pl.BlockSpec(memory_space=pltpu.HBM)
    nsem = 26 + 8
    shapes = (
        jax.ShapeDtypeStruct((NVEC, HALF), F32),
        jax.ShapeDtypeStruct((NVEC, HALF), F32),
        jax.ShapeDtypeStruct((3, NVEC), F32),
        jax.ShapeDtypeStruct((KR * BANDS, FINE * BANDS), BF16),
    )
    operands = (interp_map.T, coarse_kernel, interp_coef, energy.reshape(1, HALF), start_vectors)
    results = pl.pallas_call(
        kernel,
        out_shape=shapes,
        in_specs=[hbm] * 5,
        out_specs=(vmem, vmem, vmem, vmem),
        scratch_shapes=[
            pltpu.SMEM((2, COLS * FINE), jnp.int32),
            pltpu.VMEM((1, 2, BANDS, BANDS), BF16),
            pltpu.VMEM((FINE, 2, BANDS, BANDS), BF16),
            pltpu.VMEM((1, HALF), F32),
            pltpu.VMEM((NVEC, HALF), F32),
            pltpu.VMEM((16, VS, HALF), F32),
            pltpu.VMEM((16, 1, HALF), F32),
            pltpu.VMEM((12, BANDS, BANDS), BF16),
            pltpu.VMEM((4, 2, BANDS, BANDS), BF16),
            pltpu.VMEM((KR, 2, BANDS, BANDS), BF16),
            pltpu.VMEM((KR, 2, BANDS, BANDS), BF16),
            pltpu.VMEM((4, KR * BANDS, BANDS), BF16),
            pltpu.VMEM((2, VS, 2 * BANDS), BF16),
            pltpu.VMEM((2, 2, VS, BANDS), BF16),
            pltpu.VMEM((2, 2, VS, BANDS), BF16),
            pltpu.VMEM((2, ROWS, VS, 2 * BANDS), BF16),
            pltpu.VMEM((2, ROWS, VS, BANDS), BF16),
            pltpu.VMEM((4 * COLS, VS, BANDS), BF16),
            pltpu.VMEM((4, 1, HALF), F32),
            pltpu.VMEM((COLS, 4, 1, HALF), F32),
            pltpu.VMEM((5, 1, HALF), F32),
            pltpu.VMEM((ROWS, 5, 1, HALF), F32),
            pltpu.VMEM((16, VS, HALF), BF16),
            pltpu.VMEM((16, VS, HALF), BF16),
            pltpu.VMEM((COLS, 2, VS, BANDS), BF16),
            pltpu.VMEM((2, VS, BANDS), BF16),
            pltpu.VMEM((2 * VS, BANDS), BF16),
            pltpu.VMEM((2, 2 * VS, BANDS), BF16),
            pltpu.VMEM((COLS, 2 * VS, HALF), BF16),
            pltpu.VMEM((COLS, 2 * VS, HALF), BF16),
            pltpu.VMEM((1, HALF), F32),
            pltpu.VMEM((COLS * ROWS, 1, HALF), F32),
            pltpu.SemaphoreType.DMA((nsem,)),
            pltpu.SemaphoreType.DMA((nsem,)),
            pltpu.SemaphoreType.DMA((5,)),
        ],
        compiler_params=pltpu.CompilerParams(
            has_side_effects=True, collective_id=0, vmem_limit_bytes=40 * 1024 * 1024
        ),
    )(*(pltpu.with_memory_space_constraint(v, pltpu.HBM) for v in operands))
    return pl.pallas_call(
        write_out,
        out_shape=shapes,
        in_specs=[vmem] * 4,
        out_specs=(hbm,) * 4,
        scratch_shapes=[pltpu.SemaphoreType.DMA((11,))],
        compiler_params=pltpu.CompilerParams(vmem_limit_bytes=1024 * 1024),
    )(*results)


def solution(mesh):
    return jax.shard_map(
        per_device,
        mesh=mesh,
        in_specs=(
            P("row", "col", None, None),
            P("col", None, None, None),
            P(),
            P(("row", "col")),
            P(None, ("row", "col")),
        ),
        out_specs=(P(None, ("row", "col")), P(None, ("row", "col")), P(), P("row", "col")),
        check_vma=False,
    )
```

```python
import jax
import jax.numpy as jnp
from jax import lax
from jax.experimental import pallas as pl
from jax.experimental.pallas import tpu as pltpu
from jax.sharding import PartitionSpec as P

ROWS = 16
COLS = 8
BANDS = 256
NVEC = 256
FINE = 8
KR = 4
VS = NVEC // ROWS
HALF = 128
ORDER = 16384
EPS = 1e-06
PRESCALE = 0.125
SHIFT = 2.0

F32 = jnp.float32
BF16 = jnp.bfloat16
MESH = pl.DeviceIdType.MESH

NT = (((1,), (1,)), ((), ()))
NN = (((1,), (0,)), ((), ()))

OFFSETS = sorted(
    ((dy, dx) for dy in range(4) for dx in range(4)),
    key=lambda t: -(min(t[0], 4 - t[0]) + min(t[1], 4 - t[1])),
)
AROUND = (4, 2, 6, 3, 5, 1, 7, 0)


def groups():
    steps = {t: min(t[0], 4 - t[0]) + min(t[1], 4 - t[1]) for t in OFFSETS}
    return [[t for t in OFFSETS if low <= steps[t] <= high] for low, high in ((0, 1), (2, 2), (3, 4))]


GROUPS = groups()


def mm(a, b, dims):
    return lax.dot_general(a, b, dims, preferred_element_type=F32)


def wait_bytes(ref, sem):
    pltpu.make_async_copy(ref, ref, sem).wait()


def kernel(
    map_hbm, kc_hbm, coef_hbm, e_hbm, s_hbm,
    second_ref, resid_ref, coeffs_ref, tile_ref,
    map_ref, kc_ref, coef_ref, e_ref, s_ref,
    scol, ecol, kbuf, cj, ci, cit, lbuf,
    wsend, wside, wnear, wfull, usend, ured,
    zs_send, zs_recv, ab_send, ab_recv, y_send, y_nat, zred, wdot, usum, uside, z_send, z_nat, dot_send, dot_recv,
    ssem, rsem, lsem,
):
    r = lax.axis_index("row")
    c = lax.axis_index("col")
    z = lax.div(c, 2)
    k = lax.rem(c, 2)
    x = lax.rem(r, 4)
    y = lax.div(r, 4)
    odd = lax.rem(r, 2)
    c_prev = lax.rem(c + COLS - 1, COLS)
    c_next = lax.rem(c + 1, COLS)
    diag_col = lax.div(r, 2)
    near_col = lax.rem(diag_col + COLS - 1 + 2 * odd, COLS)
    is_diag = c == diag_col
    is_near = c == near_col
    first_row = 2 * c
    away = lax.rem(z - y + 4, 4)
    r_next = lax.rem(r + 1, ROWS)
    r_prev = lax.rem(r + ROWS - 1, ROWS)
    sibling = 2 * z + (1 - k)
    finish = []

    loads = []
    for n, (src, dst) in enumerate(((s_hbm, s_ref), (e_hbm, e_ref), (kc_hbm, kc_ref), (coef_hbm, coef_ref), (map_hbm, map_ref))):
        loads.append(pltpu.make_async_copy(src, dst, lsem.at[n]))
        loads[-1].start()

    barrier = pltpu.get_barrier_semaphore()

    def greet(tr, tc):
        pl.semaphore_signal(barrier, inc=1, device_id=(tr, tc), device_id_type=MESH)

    def plane_row(t):
        dy, dx = t
        return 4 * lax.rem(y + dy, 4) + lax.rem(x + dx, 4)

    for q in range(ROWS):
        tr, tc = first_row + q // COLS, q % COLS

        @pl.when(jnp.logical_not(jnp.logical_and(tr == r, tc == c)))
        def _(tr=tr, tc=tc):
            greet(tr, tc)

    for t in range(1, COLS):
        greet(r, lax.rem(c + t, COLS))
    greet(r_next, c)
    greet(r_prev, c)
    pl.semaphore_wait(barrier, 16 + 7 + 2 - is_diag.astype(jnp.int32))

    def remote(src, dst, sem, tr, tc, out=None):
        pltpu.make_async_remote_copy(
            src_ref=src, dst_ref=dst, recv_sem=rsem.at[sem],
            send_sem=ssem.at[sem if out is None else out],
            device_id=(tr, tc), device_id_type=MESH,
        ).start()

    def local(src, dst, sem):
        pltpu.make_async_copy(src, dst, rsem.at[sem]).start()

    def either(here, src, dst, sem, tr, tc, out=None):
        @pl.when(here)
        def _():
            local(src, dst, sem)

        @pl.when(jnp.logical_not(here))
        def _():
            remote(src, dst, sem, tr, tc, out)

    def finish_plain(sem, buf):
        finish.append(lambda: wait_bytes(buf, ssem.at[sem]))

    def finish_but_one(here, sem, buf, count):
        def run():
            @pl.when(here)
            def _():
                wait_bytes(buf.at[pl.ds(0, count - 1)], ssem.at[sem])

            @pl.when(jnp.logical_not(here))
            def _():
                wait_bytes(buf.at[pl.ds(0, count)], ssem.at[sem])

        finish.append(run)

    E, K2, CB, AB, YN, WD, UN, ZN, DOT, ZS = range(10)
    K1, C1, C3, S, HW, APP = 10, 12, 16, 20, 24, 26

    loads[0].wait()
    loads[1].wait()
    for t in OFFSETS:
        tr = plane_row(t)
        src = s_ref.at[pl.ds(pl.multiple_of(tr * VS, VS), VS), :]
        dst = scol.at[odd * COLS + c]
        if t == (0, 0):
            either(is_diag, src, dst, S + away, tr, diag_col, S)
        else:
            remote(src, dst, S + away, tr, diag_col, S)
    finish_but_one(is_diag, S, scol, ROWS)
    for t in OFFSETS:
        tr = plane_row(t)
        dst = ecol.at[odd * COLS + c]
        if t == (0, 0):
            either(is_diag, e_ref, dst, E, tr, diag_col)
        else:
            remote(e_ref, dst, E, tr, diag_col)
    finish_but_one(is_diag, E, ecol, ROWS)
    loads[2].wait()
    loads[3].wait()
    loads[4].wait()

    delta = lax.rem(y - z + 4, 4)
    mine = lax.rem(x, 2) * KR + delta
    home_core = lax.div(x, 2)
    at_source = delta == 0
    serves = k == home_core
    is_home = jnp.logical_and(at_source, serves)
    pair = pl.ds(2 * k, 2)
    piece = [lax.rem(delta + t, 4) for t in range(4)]
    holds = [lax.div(p, 2) == k for p in piece]

    def ring_col(t, core):
        return 2 * lax.rem(z + t, 4) + core

    def row_blocks(b):
        remote(kc_ref.at[0, b], kbuf.at[1 + b], K1 + b, r_next, c)
        remote(kc_ref.at[0, b], kbuf.at[9 + b], K1 + b, r_prev, c)

    def column_blocks(b):
        wait_bytes(kbuf.at[pl.ds(0, 2)], rsem.at[K1 + b])
        for slot in range(3):
            if b == 0:
                remote(kbuf.at[4 * slot + 1], kbuf.at[4 * slot + 3], K2, r, c_prev)
            else:
                remote(kbuf.at[4 * slot + 2], kbuf.at[4 * slot], K2, r, c_next)

    def bulk_first():
        @pl.when(serves)
        def _():
            for t in (1, 3):
                remote(coef_ref.at[mine], cj.at[t], C1 + t, r, ring_col(t, lax.div(delta, 2)), C1)

    def bulk_second():
        for t in (1, 3):
            @pl.when(holds[t])
            def _(t=t):
                wait_bytes(cj.at[t], rsem.at[C1 + t])
                n = t // 2
                remote(cj.at[t, n], cj.at[2, n], C1 + 2, r, ring_col(t, k), C1 + t)

        column_blocks(0)

    def bulk_third():
        row_blocks(1)

        @pl.when(holds[2])
        def _():
            wait_bytes(cj.at[2], rsem.at[C1 + 2])

        for t in (1, 2, 3):
            @pl.when(jnp.logical_and(holds[t], lax.rem(piece[t], 2) == 1))
            def _(t=t):
                remote(cj.at[t], ci.at[piece[t]], C3, 4 * lax.rem(z + 4 - t, 4) + x, c, C3 + t)

            @pl.when(jnp.logical_and(holds[t], piece[t] == 0))
            def _(t=t):
                local(cj.at[t], ci.at[0], C3)

        far_piece(0)

    def far_piece(n):
        for t in (1, 2, 3):
            @pl.when(jnp.logical_and(holds[t], piece[t] == 2))
            def _(t=t):
                remote(cj.at[t, n], ci.at[2, n], C3, 4 * lax.rem(z + 4 - t, 4) + x, c, C3 + t)

    def bulk_siblings():
        @pl.when(jnp.logical_not(at_source))
        def _():
            wait_bytes(ci.at[pl.ds(0, 2)], rsem.at[C3])
            remote(ci.at[pair], ci.at[pair], CB, r, sibling)

        @pl.when(is_home)
        def _():
            src = coef_ref.at[pl.ds(odd * KR, KR)]
            local(src, ci, C1)
            remote(src, ci, CB, r, sibling)

    def bulk_wait():
        @pl.when(is_home)
        def _():
            wait_bytes(ci, rsem.at[C1])

        @pl.when(jnp.logical_not(at_source))
        def _():
            wait_bytes(ci.at[pl.ds(0, 2)], rsem.at[CB])

        @pl.when(jnp.logical_and(at_source, k != home_core))
        def _():
            wait_bytes(ci, rsem.at[CB])

        wait_bytes(kbuf.at[pl.ds(0, 6)], rsem.at[K2])

    def bulk_finish():
        wait_bytes(kbuf.at[pl.ds(0, 2)], ssem.at[K1])
        wait_bytes(kbuf.at[pl.ds(0, 2)], ssem.at[K1 + 1])
        wait_bytes(kbuf.at[pl.ds(0, 6)], ssem.at[K2])

        @pl.when(serves)
        def _():
            wait_bytes(ci.at[pl.ds(0, 2)], ssem.at[C1])

        for t in (1, 3):
            @pl.when(holds[t])
            def _(t=t):
                wait_bytes(kbuf.at[0], ssem.at[C1 + t])

        for t in (1, 2, 3):
            @pl.when(jnp.logical_and(holds[t], piece[t] != 0))
            def _(t=t):
                wait_bytes(ci.at[0], ssem.at[C3 + t])

        @pl.when(jnp.logical_not(at_source))
        def _():
            wait_bytes(ci.at[pl.ds(0, 2)], ssem.at[CB])

        @pl.when(is_home)
        def _():
            wait_bytes(ci, ssem.at[CB])

    finish.append(bulk_finish)
    bulk_first()
    for b in range(2):
        kbuf[5 + b] = kc_ref[0, b]

    plus = []
    for j in range(FINE):
        home = c * 2 + j // KR
        flag = map_ref[1, c * FINE + j] == lax.rem(home + 1, ROWS)
        plus.append(flag.astype(F32))

    def split(v):
        high = v.astype(BF16)
        return high, (v - high.astype(F32)).astype(BF16)

    def restrict_first():
        acc = [None] * 4

        def add(h, v):
            acc[h] = v if acc[h] is None else acc[h] + v

        for step in (0, 1, 3, 2):
            wait_bytes(scol.at[pl.ds(0, 4)], rsem.at[S + step])
            if step == 0:
                row_blocks(0)
            place_in = lax.rem(z + step, 4)
            for h in range(2):
                j = KR * h + place_in
                value = jnp.concatenate([scol[2 * j], scol[2 * j + 1]], axis=1) * PRESCALE
                both = jnp.concatenate(split(value), axis=0)
                flag = map_ref[1, c * FINE + j] == lax.rem(c * 2 + h + 1, ROWS)
                up = both * flag.astype(F32).astype(BF16)
                add(1 + h, mm(both, coef_ref[j, 0], NT))
                side = mm(jnp.concatenate([both - up, up], axis=0), coef_ref[j, 1], NT)
                add(h, side[:2 * VS])
                add(2 + h, side[2 * VS:])
        spread(acc, 0)

    def restrict(parts, app):
        acc = [None] * 4

        def add(h, v):
            acc[h] = v if acc[h] is None else acc[h] + v

        for j in range(FINE):
            home = 1 + j // KR
            both = jnp.concatenate(split(parts[j]), axis=0)
            add(home, mm(both, coef_ref[j, 0], NT))
            if j % KR == 0:
                add(home - 1, mm(both, coef_ref[j, 1], NT))
            elif j % KR == KR - 1:
                add(home + 1, mm(both, coef_ref[j, 1], NT))
            else:
                up = both * plus[j].astype(BF16)
                side = mm(jnp.concatenate([both - up, up], axis=0), coef_ref[j, 1], NT)
                add(home - 1, side[:2 * VS])
                add(home + 1, side[2 * VS:])
        spread(acc, app)

    def spread(acc, app):
        acc = [v[:VS] + v[VS:] for v in acc]
        sem = HW + app
        wside[app, 0] = acc[0].astype(BF16)
        wside[app, 1] = acc[3].astype(BF16)
        remote(wside.at[app, 0], wnear.at[app, 1], sem, r, c_prev)
        remote(wside.at[app, 1], wnear.at[app, 0], sem, r, c_next)
        finish_plain(sem, wside.at[app])
        wait_bytes(wnear.at[app], rsem.at[sem])
        total = [acc[1 + h] + wnear[app, h].astype(F32) for h in range(2)]
        wsend[app] = jnp.concatenate(total, axis=1).astype(BF16)
        for g in (2, 1, 0):
            sem = APP + 4 * app + g
            for t in GROUPS[g]:
                if t == (0, 0):
                    local(wsend.at[app], wfull.at[app, r], sem)
                else:
                    remote(wsend.at[app], wfull.at[app, r], sem, plane_row(t), c)
            finish_plain(sem, wfull.at[app, pl.ds(0, len(GROUPS[g]) - (g == 0))])

    def coarse_apply(app):
        sem = APP + 4 * app + 3
        for g, group in enumerate(GROUPS):
            wait_bytes(wfull.at[app, pl.ds(0, len(group))], rsem.at[APP + 4 * app + g])
            slots = [plane_row(t) for t in group]
            own = jnp.concatenate([wfull[app, tr] for tr in slots], axis=0)
            part = mm(own[:, :BANDS], kc_ref[0, 0], NT) + mm(own[:, BANDS:], kc_ref[0, 1], NT)
            part = part.astype(BF16)
            for n, tr in enumerate(slots):
                usend[app, tr] = part[n * VS:(n + 1) * VS]
            for t, tr in zip(group, slots):
                src = usend.at[app, tr]
                if app:
                    half = lax.div(tr, 2)
                    either(half == c, src, zred.at[c, lax.rem(tr, 2)], sem, r, half)
                    continue
                own = ured.at[(1 + odd) * COLS + c]
                near = ured.at[3 * (1 - odd) * COLS + c]
                if t == (0, 0):
                    either(is_diag, src, own, sem, tr, diag_col)
                    either(is_near, src, near, sem, tr, near_col)
                else:
                    remote(src, own, sem, tr, diag_col)
                    remote(src, near, sem, tr, near_col)
        if app:
            finish_plain(sem, usend.at[app, pl.ds(0, ROWS - 2)])
        else:
            finish_but_one(jnp.logical_or(is_diag, is_near), sem, ured, 4 * COLS)

    def reduce_coarse():
        wait_bytes(ured, rsem.at[APP + 3])
        u = []
        for h in range(4):
            total = ured[h * COLS].astype(F32)
            for t in range(1, COLS):
                total = total + ured[h * COLS + t].astype(F32)
            u.append(jnp.concatenate(split(total), axis=0))
        return u

    def prolong(u, j):
        home = 1 + j // KR
        if j % KR == 0:
            side = u[home - 1]
        elif j % KR == KR - 1:
            side = u[home + 1]
        else:
            up, down = plus[j].astype(BF16), (1.0 - plus[j]).astype(BF16)
            side = u[home - 1] * down + u[home + 1] * up
        value = mm(u[home], coef_ref[j, 0], NN) + mm(side, coef_ref[j, 1], NN)
        return value[:VS] + value[VS:]

    def to_native(src, dst, sem):
        for t in OFFSETS:
            dy, dx = t
            q = lax.rem(odd * COLS + c + 4 * dy + dx, ROWS)
            tr = first_row + lax.div(q, COLS)
            tc = lax.rem(q, COLS)
            if t == (0, 0):
                either(is_diag, src.at[q], dst.at[r], sem, tr, tc)
            else:
                remote(src.at[q], dst.at[r], sem, tr, tc)
        finish_but_one(is_diag, sem, src, ROWS)

    lanes = lax.broadcasted_iota(jnp.int32, (VS, HALF), 1)
    vecs = lax.broadcasted_iota(jnp.int32, (VS, HALF), 0)

    def place(shift):
        return lanes == vecs + VS * shift

    own_place = place(lax.rem(r, 8))

    lane_group = lax.div(lax.broadcasted_iota(jnp.int32, (1, HALF), 1), VS)

    def place_row(shift):
        return lane_group == shift

    def as_row(v):
        return jnp.sum(jnp.where(own_place, v, 0.0), axis=0, keepdims=True)

    def as_column(row, mask):
        return jnp.sum(jnp.where(mask, row, 0.0), axis=1, keepdims=True)

    def s_block(j):
        return jnp.concatenate([scol[2 * j], scol[2 * j + 1]], axis=1) * PRESCALE

    def d_block(j):
        return jnp.concatenate([ecol[2 * j], ecol[2 * j + 1]], axis=1) - SHIFT

    def keep(buf, j, v):
        for h in range(2):
            buf[2 * j + h] = v[:, h * HALF:(h + 1) * HALF].astype(BF16)

    def row_sum(v):
        return jnp.sum(v, axis=1, keepdims=True)

    def left_part():
        for i in range(KR):
            for n in range(2):
                cit[i, n] = ci[i, n].T
        for i in range(KR):
            flag = map_ref[1, r * KR + i] == r_next
            row = jnp.where(flag, 8, 0)
            for b in range(4):
                value = mm(cit[i, 0], kbuf[4 + b], NN) + mm(cit[i, 1], kbuf[row + b], NN)
                lbuf[b, pl.ds(i * BANDS, BANDS), :] = value.astype(BF16)

    def tile_piece(j):
        home = 1 + j // KR
        flag = map_ref[1, c * FINE + j] == lax.rem(c * 2 + j // KR + 1, ROWS)
        other = jnp.where(flag, home + 1, home - 1)
        for m in range(KR):
            rows = pl.ds(m * BANDS, BANDS)
            value = mm(lbuf[home, rows], coef_ref[j, 0], NN) + mm(lbuf[other, rows], coef_ref[j, 1], NN)
            tile_ref[rows, pl.ds(j * BANDS, BANDS)] = value.astype(BF16)

    restrict_first()
    bulk_second()
    coarse_apply(0)
    bulk_third()
    u = reduce_coarse()
    wait_bytes(ecol, rsem.at[E])
    parts = []
    ss = sg = gg = gdg = jnp.zeros((VS, 1), F32)
    for j in range(FINE):
        s_j = s_block(j)
        y_j = prolong(u, j)
        g_j = y_j + d_block(j) * s_j
        parts.append(g_j)
        keep(y_send, j, y_j)
        ss = ss + row_sum(s_j * s_j)
        sg = sg + row_sum(s_j * g_j)
        gg = gg + row_sum(g_j * g_j)
        gdg = gdg + row_sum(g_j * g_j * d_block(j))

    restrict(parts, 1)
    for h in range(2):
        src = wsend.at[1, :, pl.ds(h * BANDS, BANDS)]
        either(jnp.logical_and(is_diag, odd == h), src, wdot.at[odd], WD, first_row + h, diag_col)
    finish_but_one(is_diag, WD, wdot, 2)
    for n, v in enumerate((ss, sg, gg, gdg)):
        zs_send[n] = as_row(v)
    local(zs_send, zs_recv.at[c], ZS)
    for t in range(1, COLS):
        remote(zs_send, zs_recv.at[c], ZS, r, lax.rem(c + t, COLS))
    finish_plain(ZS, zs_recv.at[pl.ds(0, COLS - 1)])
    column_blocks(1)
    far_piece(1)
    wait_bytes(zs_recv, rsem.at[ZS])
    mean = zs_recv[0]
    for t in range(1, COLS):
        mean = mean + zs_recv[t]
    mean = mean / ORDER
    ss, sg, gg, gdg = (as_column(mean[n], own_place) for n in range(4))
    var = ss + EPS * PRESCALE * PRESCALE
    scale = jnp.sqrt(var)
    alpha_one = (sg + SHIFT * ss) / var
    mix = SHIFT - alpha_one
    remain_sq = (gg + 2.0 * mix * sg + mix * mix * ss) / var
    beta = jnp.sqrt(jnp.maximum(remain_sq, 0.0) + EPS)
    inv = 1.0 / (scale * beta)
    over = beta / scale
    sec_sec = (gg + 2.0 * mix * sg + mix * mix * ss) * inv * inv
    known = (gdg + 2.0 * mix * gg + mix * mix * sg) * inv * inv + SHIFT * sec_sec
    known = known - over * inv * (sg + mix * ss)
    for n, v in enumerate((alpha_one, beta, inv, over, known)):
        ab_send[n] = as_row(v)
    bulk_siblings()
    coarse_apply(1)
    for t in OFFSETS:
        if t == (0, 0):
            local(ab_send, ab_recv.at[r], AB)
        else:
            remote(ab_send, ab_recv.at[r], AB, plane_row(t), c)
    finish_plain(AB, ab_recv.at[pl.ds(0, ROWS - 1)])
    to_native(y_send, y_nat, YN)
    bulk_wait()
    left_part()

    wait_bytes(zred, rsem.at[APP + 7])
    wait_bytes(wdot, rsem.at[WD])
    line, own_u = None, []
    for h in range(2):
        total = zred[0, h].astype(F32)
        for t in range(1, COLS):
            total = total + zred[t, h].astype(F32)
        own_u.append(total)
        usum[pl.ds(h * VS, VS), :] = total.astype(BF16)
        inner = row_sum(total * wdot[h].astype(F32))
        row = jnp.sum(jnp.where(place(2 * lax.rem(c, 4) + h), inner, 0.0), axis=0, keepdims=True)
        line = row if line is None else line + row
    remote(usum, uside.at[0], UN, r_next, c)
    remote(usum, uside.at[1], UN, r_prev, c)
    finish_plain(UN, uside)
    own_u = jnp.concatenate(split(jnp.concatenate(own_u, axis=0)), axis=0)
    dot_send[...] = line
    for tz in AROUND:
        for t in OFFSETS:
            if t == (0, 0) and tz == 0:
                local(dot_send, dot_recv.at[c * ROWS + r], DOT)
            else:
                remote(dot_send, dot_recv.at[c * ROWS + r], DOT, plane_row(t), lax.rem(c + tz, COLS))
    finish_plain(DOT, dot_recv.at[pl.ds(0, ROWS * COLS - 1)])

    for j in range(4):
        tile_piece(j)
    wait_bytes(uside, rsem.at[UN])
    for i in range(KR):
        if i == 0:
            side = uside[0]
        elif i == KR - 1:
            side = uside[1]
        else:
            up = (map_ref[1, r * KR + i] == r_next).astype(F32)
            side = uside[0] * (1.0 - up).astype(BF16) + uside[1] * up.astype(BF16)
        value = mm(own_u, ci[i, 0], NN)
        value = value[:2 * VS] + value[2 * VS:] + mm(side, ci[i, 1], NN)
        for h in range(2):
            z_send[2 * i + h] = value[:, h * HALF:(h + 1) * HALF].astype(BF16)
    for tz in AROUND:
        tc = lax.rem(c + tz, COLS)
        if tz == 0:
            local(z_send.at[tc], z_nat.at[c], ZN)
        else:
            remote(z_send.at[tc], z_nat.at[c], ZN, r, tc)
    finish_plain(ZN, z_send.at[pl.ds(0, COLS - 1)])
    for j in range(4, FINE):
        tile_piece(j)

    wait_bytes(y_nat, rsem.at[YN])
    wait_bytes(ab_recv, rsem.at[AB])
    diag = e_ref[...] - SHIFT
    for i in range(ROWS):
        rows = pl.ds(i * VS, VS)
        mask = place(i % 8)
        first = s_ref[rows, :] * PRESCALE
        image = y_nat[i].astype(F32) + diag * first
        mix_i = SHIFT - as_column(ab_recv[i, 0], mask)
        inv_i = as_column(ab_recv[i, 2], mask)
        over_i = as_column(ab_recv[i, 3], mask)
        sec = (image + mix_i * first) * inv_i
        second_ref[rows, :] = sec
        resid_ref[rows, :] = (diag * image + mix_i * image) * inv_i + SHIFT * sec - over_i * first
    wait_bytes(z_nat, rsem.at[ZN])
    image_two = z_nat[...].reshape(NVEC, HALF).astype(F32)
    wait_bytes(dot_recv, rsem.at[DOT])
    inner = []
    for h in range(2):
        total = dot_recv[h * 4 * ROWS]
        for t in range(1, 4 * ROWS):
            total = total + dot_recv[h * 4 * ROWS + t]
        inner.append(total / ORDER)

    def second_alpha(i):
        inv_row = ab_recv[i, 2]
        return ab_recv[i, 4] + jnp.where(place_row(i % 8), inner[i // 8], 0.0) * inv_row * inv_row

    alpha_two = [second_alpha(i) for i in range(ROWS)]
    lines = []
    for get in (lambda i: ab_recv[i, 0], lambda i: ab_recv[i, 1], lambda i: alpha_two[i]):
        halves = []
        for h in range(2):
            value = get(8 * h)
            for i in range(1, 8):
                value = value + get(8 * h + i)
            halves.append(value)
        lines.append(jnp.concatenate(halves, axis=1))
    coeffs_ref[...] = jnp.concatenate(lines, axis=0)
    for i in range(ROWS):
        rows = pl.ds(i * VS, VS)
        mask = place(i % 8)
        column = as_column(alpha_two[i], mask)
        inv_i = as_column(ab_recv[i, 2], mask)
        resid_ref[rows, :] = resid_ref[rows, :] + image_two[i * VS:(i + 1) * VS] * inv_i - column * second_ref[rows, :]

    for run in finish:
        run()


def write_out(*refs):
    sems = refs[8]
    copies = [pltpu.make_async_copy(refs[n], refs[4 + n], sems.at[n]) for n in range(3)]
    for n in range(8):
        rows = pl.ds(n * 128, 128)
        copies.append(pltpu.make_async_copy(refs[3].at[rows], refs[7].at[rows], sems.at[3 + n]))
    for copy in copies:
        copy.start()
    for copy in copies:
        copy.wait()


def per_device(coarse_kernel, interp_coef, interp_map, energy, start_vectors):
    vmem = pl.BlockSpec(memory_space=pltpu.VMEM)
    hbm = pl.BlockSpec(memory_space=pltpu.HBM)
    nsem = 26 + 8
    shapes = (
        jax.ShapeDtypeStruct((NVEC, HALF), F32),
        jax.ShapeDtypeStruct((NVEC, HALF), F32),
        jax.ShapeDtypeStruct((3, NVEC), F32),
        jax.ShapeDtypeStruct((KR * BANDS, FINE * BANDS), BF16),
    )
    operands = (interp_map.T, coarse_kernel, interp_coef, energy.reshape(1, HALF), start_vectors)
    results = pl.pallas_call(
        kernel,
        out_shape=shapes,
        in_specs=[hbm] * 5,
        out_specs=(vmem, vmem, vmem, vmem),
        scratch_shapes=[
            pltpu.SMEM((2, COLS * FINE), jnp.int32),
            pltpu.VMEM((1, 2, BANDS, BANDS), BF16),
            pltpu.VMEM((FINE, 2, BANDS, BANDS), BF16),
            pltpu.VMEM((1, HALF), F32),
            pltpu.VMEM((NVEC, HALF), F32),
            pltpu.VMEM((16, VS, HALF), F32),
            pltpu.VMEM((16, 1, HALF), F32),
            pltpu.VMEM((12, BANDS, BANDS), BF16),
            pltpu.VMEM((4, 2, BANDS, BANDS), BF16),
            pltpu.VMEM((KR, 2, BANDS, BANDS), BF16),
            pltpu.VMEM((KR, 2, BANDS, BANDS), BF16),
            pltpu.VMEM((4, KR * BANDS, BANDS), BF16),
            pltpu.VMEM((2, VS, 2 * BANDS), BF16),
            pltpu.VMEM((2, 2, VS, BANDS), BF16),
            pltpu.VMEM((2, 2, VS, BANDS), BF16),
            pltpu.VMEM((2, ROWS, VS, 2 * BANDS), BF16),
            pltpu.VMEM((2, ROWS, VS, BANDS), BF16),
            pltpu.VMEM((4 * COLS, VS, BANDS), BF16),
            pltpu.VMEM((4, 1, HALF), F32),
            pltpu.VMEM((COLS, 4, 1, HALF), F32),
            pltpu.VMEM((5, 1, HALF), F32),
            pltpu.VMEM((ROWS, 5, 1, HALF), F32),
            pltpu.VMEM((16, VS, HALF), BF16),
            pltpu.VMEM((16, VS, HALF), BF16),
            pltpu.VMEM((COLS, 2, VS, BANDS), BF16),
            pltpu.VMEM((2, VS, BANDS), BF16),
            pltpu.VMEM((2 * VS, BANDS), BF16),
            pltpu.VMEM((2, 2 * VS, BANDS), BF16),
            pltpu.VMEM((COLS, 2 * VS, HALF), BF16),
            pltpu.VMEM((COLS, 2 * VS, HALF), BF16),
            pltpu.VMEM((1, HALF), F32),
            pltpu.VMEM((COLS * ROWS, 1, HALF), F32),
            pltpu.SemaphoreType.DMA((nsem,)),
            pltpu.SemaphoreType.DMA((nsem,)),
            pltpu.SemaphoreType.DMA((5,)),
        ],
        compiler_params=pltpu.CompilerParams(
            has_side_effects=True, collective_id=0, vmem_limit_bytes=40 * 1024 * 1024
        ),
    )(*(pltpu.with_memory_space_constraint(v, pltpu.HBM) for v in operands))
    return pl.pallas_call(
        write_out,
        out_shape=shapes,
        in_specs=[vmem] * 4,
        out_specs=(hbm,) * 4,
        scratch_shapes=[pltpu.SemaphoreType.DMA((11,))],
        compiler_params=pltpu.CompilerParams(vmem_limit_bytes=1024 * 1024),
    )(*results)


def solution(mesh):
    return jax.shard_map(
        per_device,
        mesh=mesh,
        in_specs=(
            P("row", "col", None, None),
            P("col", None, None, None),
            P(),
            P(("row", "col")),
            P(None, ("row", "col")),
        ),
        out_specs=(P(None, ("row", "col")), P(None, ("row", "col")), P(), P("row", "col")),
        check_vma=False,
    )
```
